256 devices in a mesh: trow: 4 (over y), tcol: 4 (over x), pix: 16 (over z, core).
Axes of the slice: x: 4, y: 4, z: 8, core: 2. Of those that a mesh axis runs over, the one named last changes fastest.
Arguments:
- frames: float32 [6144, 2, 64, 128], P(('trow', 'tcol'), None, 'pix'), may hold values from 0.1 to 8
- drift: int32 [6144, 2], P(('trow', 'tcol')), may hold values from -7 to 7
Outputs:
- inner_cycle: float32 [6144, 6144], P(('trow', 'pix'), 'tcol')
- second_band_twotime: float32 [6144, 6144], P(('trow', 'pix'), 'tcol')
The draws below stay inside these ranges and needn't reach their ends.
All inputs are finite; a program needn't handle non-finite values.
Results may differ from the reference program's by a relative error of at most 0.0003.
Values may be sent and summed in bfloat16 or wider, within the bound.
A program may use at most 128 MiB of HBM per device.

```python
import math
import jax
import jax.numpy as jnp
from jax import lax

RB = 64
COLS = 128
EXPOSURE_TALLY = 6144
PB = 8192


def draw_frames(key, part):
    pixel_shape = (2, RB, COLS)
    key_pixel = jax.random.fold_in(key, 101)
    key_frame = jax.random.fold_in(key, 102)
    key_phase = jax.random.fold_in(key, 103)
    flurry_seed_handle = jax.random.fold_in(key, 104)
    key_static = jax.random.fold_in(key, 105)
    key_start = jax.random.fold_in(key, 106)
    key_noise = jax.random.fold_in(key, 107)
    pixel_low, pixel_high = (0.3, 3.0)
    pixel_level = jnp.exp(jax.random.uniform(key_pixel, pixel_shape, jnp.float32, math.log(pixel_low), math.log(pixel_high)))
    frame_level = jnp.exp(jax.random.uniform(key_frame, (EXPOSURE_TALLY,), jnp.float32, math.log(0.3), math.log(3.0)))
    progress = jnp.arange(EXPOSURE_TALLY, dtype=jnp.float32) / EXPOSURE_TALLY
    grain_decay_period = 40.0 * 12.5 ** progress
    phase_offset = jax.random.uniform(key_phase, (), jnp.float32, 0.0, 1.0)
    share = 0.35 + 0.3 * jnp.sin(2.0 * math.pi * (1.5 * progress + phase_offset))
    exposure_flurry_stack = jax.random.randint(flurry_seed_handle, (6,), 0, EXPOSURE_TALLY)
    flurry_enabled = jnp.any(jnp.arange(EXPOSURE_TALLY, dtype=jnp.int32)[:, None] == exposure_flurry_stack[None, :], axis=1)
    recall_store = jnp.where(flurry_enabled, 0.3, jnp.exp(-1.0 / grain_decay_period)).astype(jnp.float32)
    static_field = jax.random.normal(key_static, (2,) + pixel_shape, jnp.float32) * math.sqrt(0.5)
    start_field = jax.random.normal(key_start, (2,) + pixel_shape, jnp.float32) * math.sqrt(0.5)

    def advance(carried_state, inputs):
        frame_index, decay_rate, fraction, frame_gain = inputs
        fresh = jax.random.normal(jax.random.fold_in(key_noise, frame_index), (2,) + pixel_shape, jnp.float32) * math.sqrt(0.5)
        carried_state = decay_rate * carried_state + jnp.sqrt(1.0 - decay_rate * decay_rate) * fresh
        amplitude = jnp.sqrt(1.0 - fraction) * carried_state + jnp.sqrt(fraction) * static_field
        intensity = amplitude[0] * amplitude[0] + amplitude[1] * amplitude[1]
        return (carried_state, jnp.minimum(0.1 + 0.5 * frame_gain * pixel_level * intensity, 8.0))
    ignored, series = lax.scan(advance, start_field, (jnp.arange(EXPOSURE_TALLY, dtype=jnp.int32), recall_store, share.astype(jnp.float32), frame_level))
    return series


def plant(values, stream_key, smallest, largest):
    dims = values.shape
    spot = [jax.random.randint(jax.random.fold_in(stream_key, axis), (), 0, dims[axis]) for axis in range(len(dims))]
    values = values.at[tuple(spot)].set(smallest)
    longest = dims.index(max(dims))
    spot[longest] = (spot[longest] + 1) % dims[longest]
    return values.at[tuple(spot)].set(largest)


def setup_inputs(seed: int = 0) -> dict:
    seeds = jax.random.split(jax.random.key(seed), 3)
    frames = draw_frames(jax.random.fold_in(seeds[2], 71), 0)
    drift = plant(jax.random.randint(seeds[1], (EXPOSURE_TALLY, 2), -7, 8), jax.random.fold_in(seeds[1], 1), -7, 7).astype(jnp.int32)
    return dict(frames=frames, drift=drift)


def blend(padded, steps, device_axis):
    upward = (jnp.maximum(steps, 0).astype(jnp.float32) / 8.0)[:, None, None, None]
    downward = (jnp.maximum(-steps, 0).astype(jnp.float32) / 8.0)[:, None, None, None]
    length = padded.shape[device_axis] - 2
    middle = lax.slice_in_dim(padded, 1, 1 + length, 1, device_axis)
    after = lax.slice_in_dim(padded, 2, 2 + length, 1, device_axis)
    before = lax.slice_in_dim(padded, 0, length, 1, device_axis)
    return (1.0 - upward - downward) * middle + upward * after + downward * before


def reference(frames, drift):
    padded = jnp.pad(frames, ((0, 0), (0, 0), (1, 1), (0, 0)))
    rowpass = blend(padded, drift[:, 0], 2)
    padded = jnp.pad(rowpass, ((0, 0), (0, 0), (0, 0), (1, 1)))
    shifted = blend(padded, drift[:, 1], 3)
    pixel_mean = jnp.sum(shifted, axis=0) / EXPOSURE_TALLY
    flat = shifted / pixel_mean[None]
    frame_mean = jnp.sum(flat, axis=(2, 3)) / PB
    normed = (flat / frame_mean[:, :, None, None]).astype(jnp.bfloat16)
    results = []
    for band in range(2):
        band_data = normed[:, band].reshape(EXPOSURE_TALLY, PB).astype(jnp.float32)
        gram_full = jnp.dot(band_data, band_data.T, precision=lax.Precision.HIGHEST, preferred_element_type=jnp.float32)
        results.append(gram_full / PB)
    return results[0], results[1]
```

```python
import functools

import jax
import jax.numpy as jnp
from jax import lax
from jax.experimental import pallas as pl
from jax.experimental.pallas import tpu as pltpu
from jax.sharding import PartitionSpec as P

MESH = pl.DeviceIdType.MESH
SCALE = 32000.0
SUBS = 2


def remote(src, dst, send, recv, device):
    return pltpu.make_async_remote_copy(
        src_ref=src, dst_ref=dst, send_sem=send, recv_sem=recv, device_id=device, device_id_type=MESH
    )


def around(index, step, count):
    return lax.rem(index + step + count, count)


def edge_rows(cells, axis):
    count = lax.axis_size(axis)
    ends = count - 1
    head = lax.slice_in_dim(cells, 0, 1, axis=2)
    tail = lax.slice_in_dim(cells, cells.shape[2] - 1, cells.shape[2], axis=2)
    above = lax.ppermute(tail, axis, [(i, i + 1) for i in range(ends)])
    below = lax.ppermute(head, axis, [(i + 1, i) for i in range(ends)])
    return jnp.concatenate([above, cells, below], axis=2)


def blend(padded, steps, device_axis):
    upward = (jnp.maximum(steps, 0).astype(jnp.float32) / 8.0)[:, None, None, None]
    downward = (jnp.maximum(-steps, 0).astype(jnp.float32) / 8.0)[:, None, None, None]
    length = padded.shape[device_axis] - 2
    middle = lax.slice_in_dim(padded, 1, 1 + length, 1, device_axis)
    after = lax.slice_in_dim(padded, 2, 2 + length, 1, device_axis)
    before = lax.slice_in_dim(padded, 0, length, 1, device_axis)
    return (1.0 - upward - downward) * middle + upward * after + downward * before


def normalise_kernel(s_ref, n_ref, a_ref, px, py, pc, pz, xs, xr, ys, yr, cs, cr, zs, zr, *, frames, pixels):
    trow, tcol, pix = lax.axis_index("trow"), lax.axis_index("tcol"), lax.axis_index("pix")
    z, core = pix // 2, lax.rem(pix, 2)
    local = s_ref.shape[2]
    x_peers = [{"tcol": around(tcol, o, 4)} for o in (1, 2, 3)]
    y_peers = [{"trow": around(trow, o, 4)} for o in (1, 2, 3)]
    z_peers = [{"pix": around(pix, 2 * o, 16)} for o in range(1, 8)]
    partner = {"pix": pix + 1 - 2 * core}

    total = jnp.sum(s_ref[...], axis=2).reshape(8, 128)
    px[tcol] = total

    barrier = pltpu.get_barrier_semaphore()
    for device in [*x_peers, *y_peers, *z_peers, partner]:
        pl.semaphore_signal(barrier, inc=1, device_id=device, device_id_type=MESH)
    pl.semaphore_wait(barrier, 14)

    def exchange(slots, own, peers, send, recv):
        copies = [
            remote(slots.at[own], slots.at[own], send.at[i], recv.at[i], peer) for i, peer in enumerate(peers)
        ]
        for copy in copies:
            copy.start()
        for copy in copies:
            copy.wait()
        total = slots[0]
        for i in range(1, len(peers) + 1):
            total = total + slots[i]
        return total

    total = exchange(px, tcol, x_peers, xs, xr)
    py[trow] = total
    total = exchange(py, trow, y_peers, ys, yr)
    gain = frames / total

    lane = lax.broadcasted_iota(jnp.int32, (local, 128), 1)
    columns = jnp.zeros((local, 128), jnp.float32)
    for band in range(2):
        plain = jnp.zeros((local, 128), jnp.float32)
        square = jnp.zeros((local, 128), jnp.float32)
        for row in range(4):
            flat = s_ref[band, row] * gain[4 * band + row][None, :]
            plain = plain + flat
            square = square + flat * flat
        columns = jnp.where(lane == 2 * band, jnp.sum(plain, axis=1, keepdims=True), columns)
        columns = jnp.where(lane == 2 * band + 1, jnp.sum(square, axis=1, keepdims=True), columns)
    pc[core] = jnp.transpose(columns)[:8]
    pz[z] = exchange(pc, core, [partner], cs, cr)
    sums = exchange(pz, z, z_peers, zs, zr)

    for band in range(2):
        mean = sums[2 * band : 2 * band + 1] / pixels
        norm = jnp.sqrt(sums[2 * band + 1 : 2 * band + 2])
        a_ref[band : band + 1] = norm / mean * (1.0 / (SCALE * pixels) ** 0.5)
    wide = jnp.concatenate([sums, jnp.zeros((120, local), jnp.float32)], axis=0)
    tall = jnp.transpose(wide)
    for band in range(2):
        unit = (SCALE**0.5) / jnp.sqrt(tall[:, 2 * band + 1 : 2 * band + 2])
        for row in range(4):
            value = s_ref[band, row] * gain[4 * band + row][None, :] * unit
            n_ref[band, :, row * 128 : (row + 1) * 128] = value.astype(jnp.bfloat16)


def gram_kernel(
    n_ref, o_ref, rows, cols, gram, ring, handed,
    cs, cr, ls, xs, xr, x2s, x2r, ys, yr, yl, zs, zr, os_, or_,
):
    trow, tcol, pix = lax.axis_index("trow"), lax.axis_index("tcol"), lax.axis_index("pix")
    z, core = pix // 2, lax.rem(pix, 2)
    way = 1 - 2 * core
    local, half = n_ref.shape[1], n_ref.shape[2]
    sub = local // SUBS
    chunk = rows.shape[0] // 8
    east, west = {"tcol": around(tcol, 1, 4)}, {"tcol": around(tcol, -1, 4)}
    south, north = {"trow": around(trow, 1, 4)}, {"trow": around(trow, -1, 4)}
    onward, backward = {"pix": around(pix, 2 * way, 16)}, {"pix": around(pix, -2 * way, 16)}
    partner = {"pix": pix + 1 - 2 * core}

    barrier = pltpu.get_barrier_semaphore()
    for device in (east, west, south, north, onward, backward, partner):
        pl.semaphore_signal(barrier, inc=1, device_id=device, device_id_type=MESH)
    pl.semaphore_wait(barrier, 7)

    def piece(ref, block, u):
        return ref.at[pl.ds(pl.multiple_of(block * local + u * sub, sub), sub)]

    mine = pl.ds(pl.multiple_of(tcol * local, local), local)
    lanes = pl.ds(pl.multiple_of(core * half, half), half)
    keep = pltpu.make_async_copy(n_ref.at[core], rows.at[mine, lanes], ls)
    keep.start()
    give = remote(n_ref.at[1 - core], rows.at[mine, lanes], cs, cr, partner)
    give.start()
    keep.wait()
    give.wait()

    even, odd = range(0, SUBS, 2), range(1, SUBS, 2)

    def x_copy(d, u):
        place = piece(rows, tcol, u)
        return remote(place, place, xs.at[d, u], xr.at[d, u], (east, west)[d])

    def x2_copy(u):
        d = u % 2
        place = piece(rows, around(tcol, (-1, 1)[d], 4), u)
        return remote(place, place, x2s.at[u], x2r.at[u], (east, west)[d])

    offset = around(trow, -tcol, 4)
    place_on_path = (offset, around(0, -offset, 4))
    order = ((0, 3, 1, 2), (0, 1, 3, 2))

    def y_copies(m, u):
        d = u % 2
        block = around(tcol, order[d][m], 4)
        here, there = piece(rows, block, u), piece(cols, block, u)
        device = (south, north)[d]
        first = remote(here, there, ys.at[m, u], yr.at[m, u], device)
        later = remote(there, there, ys.at[m, u], yr.at[m, u], device)
        stay = pltpu.make_async_copy(here, there, yl.at[m, u])
        return first, later, stay

    def y_root(m):
        @pl.when(offset == 0)
        def _():
            for u in range(SUBS):
                first, _, stay = y_copies(m, u)
                first.start()
                stay.start()

    def y_relay(m):
        for u in range(SUBS):
            where = place_on_path[u % 2]

            @pl.when((where == 1) | (where == 2))
            def _():
                _, later, _ = y_copies(m, u)
                later.wait_recv()
                later.start()

    for u in (*even, *odd):
        x_copy(0, u).start()
    for u in (*odd, *even):
        x_copy(1, u).start()
    y_root(0)
    for u in range(SUBS):
        x_copy(u % 2, u).wait_recv()
        x2_copy(u).start()
    y_root(1)
    y_relay(0)
    for u in range(SUBS):
        x_copy(1 - u % 2, u).wait_recv()
    y_root(2)
    y_relay(1)
    for u in range(SUBS):
        x2_copy(u).wait_recv()
    y_root(3)
    y_relay(2)
    y_relay(3)

    for m in range(4):
        for u in range(SUBS):
            where = place_on_path[u % 2]

            @pl.when(where == 3)
            def _():
                y_copies(m, u)[1].wait_recv()

            @pl.when(where == 0)
            def _():
                y_copies(m, u)[2].wait()

    def block_of(o):
        return around(tcol, (0, 1, 3, 2)[o], 4)

    def part(ref, d):
        return ref.at[pl.ds(pl.multiple_of(d * chunk, chunk), chunk)]

    def multiply(o):
        right = cols.at[pl.ds(pl.multiple_of(block_of(o) * local, local), local)]

        def step(d, carry):
            product = lax.dot_general(
                part(rows, d)[...], right[...], (((1,), (1,)), ((), ())), preferred_element_type=jnp.float32
            )
            part(gram.at[o], d)[...] = jnp.round(product).astype(jnp.int32).astype(jnp.int16)
            return carry

        lax.fori_loop(0, 8, step, 0)

    def target(s):
        return lax.rem(z - way * (1 + s) + 16, 8)

    def z_first(o):
        return remote(part(gram.at[o], target(0)), ring.at[o, 0], zs.at[o, 0], zr.at[o, 0], onward)

    def z_next(o, s):
        return remote(ring.at[o, s - 1], ring.at[o, s], zs.at[o, s], zr.at[o, s], onward)

    def add(held, d, o):
        return (held[...].astype(jnp.int32) + part(gram.at[o], d)[...].astype(jnp.int32)).astype(jnp.int16)

    for o in range(4):
        multiply(o)
        z_first(o).start()

    def reduce_step(s, carry):
        for o in range(4):
            remote(ring.at[o, s - 1], ring.at[o, s - 1], zs.at[o, s - 1], zr.at[o, s - 1], onward).wait_recv()
            ring[o, s - 1] = add(ring.at[o, s - 1], target(s), o)
            z_next(o, s).start()
        return carry

    lax.fori_loop(1, 7, reduce_step, 0)

    def out_copy(o):
        place = o_ref.at[core, :, pl.ds(pl.multiple_of(block_of(o) * local, local), local)]
        return remote(handed.at[o, 1 - core], place, os_.at[o], or_.at[o], partner)

    def out_keep(o):
        place = o_ref.at[core, :, pl.ds(pl.multiple_of(block_of(o) * local, local), local)]
        return pltpu.make_async_copy(handed.at[o, core], place, yl.at[o, 0])

    for o in range(4):
        z_next(o, 6).wait_recv()
        final = add(ring.at[o, 6], z, o)
        handed[o, 0] = final[: chunk // 2]
        handed[o, 1] = final[chunk // 2 :]
        out_copy(o).start()
        out_keep(o).start()
    for o in range(4):
        out_keep(o).wait()
        out_copy(o).wait()

    for u in range(SUBS):
        x_copy(0, u).wait_send()
        x_copy(1, u).wait_send()
        x2_copy(u).wait_send()
        for m in range(4):
            @pl.when(place_on_path[u % 2] < 3)
            def _():
                y_copies(m, u)[1].wait_send()

    def sent(s, carry):
        for o in range(4):
            remote(ring.at[o, s], ring.at[o, s], zs.at[o, s], zr.at[o, s], onward).wait_send()
        return carry

    lax.fori_loop(0, 7, sent, 0)


def vmem(count):
    return [pl.BlockSpec(memory_space=pltpu.VMEM)] * count


def per_device(frames, drift):
    local, _, tile_rows, columns = frames.shape
    total_frames = local * lax.axis_size("trow") * lax.axis_size("tcol")
    band_pixels = tile_rows * columns * lax.axis_size("pix")
    padded = edge_rows(frames.astype(jnp.bfloat16), "pix").astype(frames.dtype)
    rowpass = blend(padded, drift[:, 0], 2)
    padded = jnp.pad(rowpass, ((0, 0), (0, 0), (0, 0), (1, 1)))
    shifted = blend(padded, drift[:, 1], 3).transpose(1, 2, 0, 3)

    dma = pltpu.SemaphoreType.DMA
    half = tile_rows * columns
    normed, amount = pl.pallas_call(
        functools.partial(normalise_kernel, frames=float(total_frames), pixels=float(band_pixels)),
        out_shape=(
            jax.ShapeDtypeStruct((2, local, half), jnp.bfloat16),
            jax.ShapeDtypeStruct((2, local), jnp.float32),
        ),
        in_specs=vmem(1),
        out_specs=tuple(vmem(2)),
        scratch_shapes=[
            pltpu.VMEM((4, 8, 128), jnp.float32),
            pltpu.VMEM((4, 8, 128), jnp.float32),
            pltpu.VMEM((2, 8, local), jnp.float32),
            pltpu.VMEM((8, 8, local), jnp.float32),
            dma((3,)), dma((3,)), dma((3,)), dma((3,)), dma((1,)), dma((1,)), dma((7,)), dma((7,)),
        ],
        compiler_params=pltpu.CompilerParams(collective_id=0, has_side_effects=True, vmem_limit_bytes=24 << 20),
        name="normalise",
    )(shifted)

    block = 4 * local
    summed = pl.pallas_call(
        gram_kernel,
        out_shape=jax.ShapeDtypeStruct((2, block // 16, block), jnp.int16),
        in_specs=vmem(1),
        out_specs=vmem(1)[0],
        scratch_shapes=[
            pltpu.VMEM((block, 2 * half), jnp.bfloat16),
            pltpu.VMEM((block, 2 * half), jnp.bfloat16),
            pltpu.VMEM((4, block, local), jnp.int16),
            pltpu.VMEM((4, 7, block // 8, local), jnp.int16),
            pltpu.VMEM((4, 2, block // 16, local), jnp.int16),
            dma, dma, dma,
            dma((2, SUBS)), dma((2, SUBS)), dma((SUBS,)), dma((SUBS,)),
            dma((4, SUBS)), dma((4, SUBS)), dma((4, SUBS)),
            dma((4, 7)), dma((4, 7)), dma((4,)), dma((4,)),
        ],
        compiler_params=pltpu.CompilerParams(collective_id=1, has_side_effects=True, vmem_limit_bytes=48 << 20),
        cost_estimate=pl.CostEstimate(flops=5 * 10**9, bytes_accessed=200 * 10**6, transcendentals=0),
        name="gram",
    )(normed)

    amounts = lax.all_gather(amount, ("trow", "tcol"), axis=0, tiled=False)
    pix = lax.axis_index("pix")
    by_block = amounts.reshape(4, 4, 2, local).transpose(0, 2, 1, 3).reshape(4, 2, block)
    right = lax.dynamic_index_in_dim(by_block, lax.axis_index("tcol"), 0, keepdims=False)
    left = lax.dynamic_index_in_dim(by_block, lax.axis_index("trow"), 0, keepdims=False)
    left = lax.dynamic_slice_in_dim(left, pix * (block // 16), block // 16, axis=1)
    return tuple(
        summed[band].astype(jnp.float32) * left[band][:, None] * right[band][None, :] for band in range(2)
    )


def solution(mesh):
    in_specs = (P(("trow", "tcol"), None, "pix", None), P(("trow", "tcol"), None))
    out_specs = (P(("trow", "pix"), "tcol"), P(("trow", "pix"), "tcol"))
    return jax.shard_map(
        per_device, mesh=mesh, in_specs=in_specs, out_specs=out_specs, check_vma=False
    )
```

```python
import functools

import jax
import jax.numpy as jnp
from jax import lax
from jax.experimental import pallas as pl
from jax.experimental.pallas import tpu as pltpu
from jax.sharding import PartitionSpec as P

MESH = pl.DeviceIdType.MESH
SCALE = 32000.0
OWN, WEST, EAST, FAR = range(4)
PATHS = (
    ((OWN, 0), (OWN, 1), (WEST, 0), (EAST, 0), (WEST, 1), (EAST, 1), (FAR, 0), (FAR, 1)),
    ((OWN, 0), (OWN, 1), (EAST, 0), (WEST, 0), (EAST, 1), (WEST, 1), (FAR, 0), (FAR, 1)),
)
STREAMS = [(0, OWN), (1, OWN), (0, WEST), (0, EAST), (1, WEST), (1, EAST), (0, FAR), (1, FAR)]


def remote(src, dst, send, recv, device):
    return pltpu.make_async_remote_copy(
        src_ref=src, dst_ref=dst, send_sem=send, recv_sem=recv, device_id=device, device_id_type=MESH
    )


def around(index, step, count):
    return lax.rem(index + step + count, count)


def twotime_kernel(
    x_ref, w_ref, o_ref,
    halo, s, give, rows, cols, gram, ring, handed, px, py, pc, pz, rsum, csum, rq, cq,
    hs, hr, pxs, pxr, pys, pyr, gs, gr, xs, xr, x2s, x2r, ys, yr, yl,
    pcs, pcr, pzs, pzr, rss, rsr, css, csr, zs, zr, os_, or_,
    *, frames, pixels,
):
    trow, tcol, pix = lax.axis_index("trow"), lax.axis_index("tcol"), lax.axis_index("pix")
    z, core = pix // 2, lax.rem(pix, 2)
    way = 1 - 2 * core
    local = x_ref.shape[2]
    sub = local // 4
    half = 4 * 128
    x_peers = [{"tcol": around(tcol, i, 4)} for i in (1, 2, 3)]
    y_peers = [{"trow": around(trow, i, 4)} for i in (1, 2, 3)]
    z_peers = [{"pix": around(pix, 2 * i, 16)} for i in range(1, 8)]
    east, west = x_peers[0], x_peers[2]
    south, north = y_peers[0], y_peers[2]
    onward = {"pix": around(pix, 2 * way, 16)}
    partner = {"pix": pix + way}
    other = {"pix": around(pix, -way, 16)}
    above, below = {"pix": around(pix, -1, 16)}, {"pix": around(pix, 1, 16)}

    barrier = pltpu.get_barrier_semaphore()
    for device in [*x_peers, *y_peers, *z_peers, partner, other]:
        pl.semaphore_signal(barrier, inc=1, device_id=device, device_id_type=MESH)
    pl.semaphore_wait(barrier, 15)

    edges = [
        remote(x_ref.at[:, 3], halo.at[0], hs.at[0], hr.at[0], below),
        remote(x_ref.at[:, 0], halo.at[1], hs.at[1], hr.at[1], above),
    ]
    for copy in edges:
        copy.start()
    for copy in edges:
        copy.wait()
    lane = lax.broadcasted_iota(jnp.int32, (sub, 128), 1)
    has_above = (pix > 0).astype(jnp.float32)
    has_below = (pix < 15).astype(jnp.float32)
    sums = [[jnp.zeros((8, 128), jnp.float32) for _ in range(4)] for _ in range(2)]
    for band in range(2):
        for t in range(4):
            at = pl.ds(t * sub, sub)
            stay_r, up_r, down_r, stay_c, up_c, down_c = (w_ref[at, i : i + 1] for i in range(6))
            up_c = jnp.where(lane < 127, up_c, 0.0)
            down_c = jnp.where(lane > 0, down_c, 0.0)
            line = [halo[0, band, at, :].astype(jnp.float32) * has_above]
            line += [x_ref[band, r, at, :].astype(jnp.float32) for r in range(4)]
            line += [halo[1, band, at, :].astype(jnp.float32) * has_below]
            for r in range(4):
                mid = stay_r * line[r + 1] + up_r * line[r + 2] + down_r * line[r]
                moved = stay_c * mid + up_c * pltpu.roll(mid, 127, 1) + down_c * pltpu.roll(mid, 1, 1)
                s[band, r, at, :] = moved
                sums[band][r] += jnp.sum(moved.reshape(sub // 8, 8, 128), axis=0)
    for band in range(2):
        for r in range(4):
            px[tcol, 4 * band + r] = jnp.sum(sums[band][r], axis=0)

    def exchange(slots, own, peers, send, recv):
        return [remote(slots.at[own], slots.at[own], send.at[i], recv.at[i], peer) for i, peer in enumerate(peers)]

    def add_up(slots, count):
        total = slots[0]
        for i in range(1, count):
            total = total + slots[i]
        return total

    def meet(slots, own, peers, send, recv):
        copies = exchange(slots, own, peers, send, recv)
        for copy in copies:
            copy.start()
        for copy in copies:
            copy.wait()
        return add_up(slots, len(peers) + 1)

    py[trow] = meet(px, tcol, x_peers, pxs, pxr)
    px[tcol] = frames / meet(py, trow, y_peers, pys, pyr)

    def gain(band, r):
        return px[tcol, pl.ds(4 * band + r, 1), :]

    def row_piece(block, e, h):
        return pl.ds(pl.multiple_of((2 * block + e) * sub, sub), sub)

    def col_piece(block, e, h):
        return pl.ds(pl.multiple_of(block * local + (2 * e + h) * sub, sub), sub)

    pieces = [(e, h) for h in range(2) for e in range(2)]
    lanes = pl.ds(pl.multiple_of(core * half, half), half)

    def give_copy(e, h):
        return remote(give.at[h, e], rows.at[h, row_piece(tcol, e, h), lanes], gs.at[h, e], gr.at[h, e], partner)

    for e, h in pieces:
        at = pl.ds((2 * e + h) * sub, sub)
        for r in range(4):
            flat = s[1 - core, r, at, :] * gain(1 - core, r)
            give[h, e, :, r * 128 : (r + 1) * 128] = flat.astype(jnp.bfloat16)
        give_copy(e, h).start()
    for e, h in pieces:
        at = pl.ds((2 * e + h) * sub, sub)
        for r in range(4):
            flat = s[core, r, at, :] * gain(core, r)
            place = pl.ds(pl.multiple_of(core * half + r * 128, 128), 128)
            rows[h, row_piece(tcol, e, h), place] = flat.astype(jnp.bfloat16)

    def x_copy(d, e, h):
        place = rows.at[h, row_piece(tcol, e, h)]
        return remote(place, place, xs.at[d, e, h], xr.at[d, e, h], (east, west)[d])

    def x2_copy(e, h):
        place = rows.at[h, row_piece(around(tcol, (-1, 1)[e], 4), e, h)]
        return remote(place, place, x2s.at[e, h], x2r.at[e, h], (east, west)[e])

    offset = around(trow, -tcol, 4)
    position = (offset, around(0, -offset, 4))

    def block_of(o):
        return around(tcol, (0, -1, 1, 2)[o], 4)

    def y_copies(d, i):
        o, h = PATHS[d][i]
        here, there = rows.at[h, row_piece(block_of(o), d, h)], cols.at[col_piece(block_of(o), d, h)]
        device = (south, north)[d]
        return here, there, device, ys.at[d, i], yr.at[d, i]

    def y_next(d, i):
        _, there, device, send, recv = y_copies(d, i)
        return remote(there, there, send, recv, device)

    def y_stay(d, i):
        here, there, _, _, _ = y_copies(d, i)
        return pltpu.make_async_copy(here, there, yl.at[d, i])

    def y_tick(tick):
        if tick < 8:
            @pl.when(offset == 0)
            def _():
                for d in range(2):
                    here, there, device, send, recv = y_copies(d, tick)
                    remote(here, there, send, recv, device).start()
                    y_stay(d, tick).start()

        for far in (1, 2):
            if 0 <= tick - far < 8:
                for d in range(2):
                    @pl.when(position[d] == far)
                    def _():
                        y_next(d, tick - far).wait_recv()
                        y_next(d, tick - far).start()

    def y_arrived(first, last):
        for i in range(first, last):
            for d in range(2):
                @pl.when(position[d] == 3)
                def _():
                    y_next(d, i).wait_recv()

                @pl.when(position[d] == 0)
                def _():
                    y_stay(d, i).wait()

    def x_start(h):
        x_copy(0, 0, h).start()
        x_copy(1, 1, h).start()
        x_copy(0, 1, h).start()
        x_copy(1, 0, h).start()

    def x_pass(h):
        for e in range(2):
            x_copy(e, e, h).wait_recv()
            x2_copy(e, h).start()

    def chunk(i, d):
        return gram.at[i, pl.ds(pl.multiple_of(d * sub, sub), sub)]

    def target(step):
        return lax.rem(z - way * (1 + step) + 16, 8)

    def multiply(i):
        h, o = STREAMS[i]
        right = cols.at[pl.ds(pl.multiple_of(block_of(o) * local, local), local)]
        scale = cq[o, 0:1]

        def step(t, carry):
            at = pl.ds(pl.multiple_of(t * 2 * sub, 2 * sub), 2 * sub)
            product = lax.dot_general(
                rows[h, at, :], right[...], (((1,), (1,)), ((), ())), preferred_element_type=jnp.float32
            )
            product = product * rq[h, at, 0:1] * scale
            gram[i, at, :] = jnp.round(product).astype(jnp.int32).astype(jnp.int16)
            return carry

        lax.fori_loop(0, 4, step, 0)
        remote(chunk(i, target(0)), ring.at[i, 0], zs.at[i, 0], zr.at[i, 0], onward).start()

    def z_copy(i, step):
        return remote(ring.at[i, step - 1], ring.at[i, step], zs.at[i, step], zr.at[i, step], onward)

    def arrived(i, step):
        remote(ring.at[i, step - 1], ring.at[i, step - 1], zs.at[i, step - 1], zr.at[i, step - 1], onward).wait_recv()

    def out_place(o, band):
        return o_ref.at[band, :, pl.ds(pl.multiple_of(block_of(o) * local, local), local)]

    def advance(i, step):
        h, o = STREAMS[i]
        arrived(i, step)
        if step < 7:
            ring[i, step - 1] = (
                ring[i, step - 1].astype(jnp.int32) + chunk(i, target(step))[...].astype(jnp.int32)
            ).astype(jnp.int16)
            z_copy(i, step).start()
            return
        final = (ring[i, 6].astype(jnp.int32) + chunk(i, z)[...].astype(jnp.int32)).astype(jnp.float32)
        at = pl.ds(pl.multiple_of(z * sub, sub), sub)
        handed[i] = final * rq[h, at, 1:2] * cq[o, 1:2]

        @pl.when(core != h)
        def _():
            remote(handed.at[i], out_place(o, core), os_.at[i], or_.at[o], partner).start()

        @pl.when(core == h)
        def _():
            pltpu.make_async_copy(handed.at[i], out_place(o, core), os_.at[i]).start()

    def frame_sums():
        wide = lax.broadcasted_iota(jnp.int32, (sub, 128), 1)
        for t in range(4):
            at = pl.ds(t * sub, sub)
            columns = jnp.zeros((sub, 128), jnp.float32)
            for band in range(2):
                plain = jnp.zeros((sub, 128), jnp.float32)
                square = jnp.zeros((sub, 128), jnp.float32)
                for r in range(4):
                    flat = s[band, r, at, :] * gain(band, r)
                    plain = plain + flat
                    square = square + flat * flat
                columns = jnp.where(wide == 2 * band, jnp.sum(plain, axis=1, keepdims=True), columns)
                columns = jnp.where(wide == 2 * band + 1, jnp.sum(square, axis=1, keepdims=True), columns)
            s[0, 0, at, :] = columns
        pc[core] = jnp.transpose(s[0, 0])[:8]

    def scales(total):
        plain = jnp.where(core == 0, total[0:1], total[2:3])
        norm = jnp.sqrt(jnp.where(core == 0, total[1:2], total[3:4]))
        quant = (SCALE**0.5) / norm
        amount = norm * (pixels / (SCALE * pixels) ** 0.5) / plain
        return jnp.concatenate([quant, amount, jnp.zeros((6, local), jnp.float32)], axis=0)

    for e, h in pieces[:2]:
        give_copy(e, h).wait_recv()
    x_start(0)
    for e, h in pieces[2:]:
        give_copy(e, h).wait_recv()
    y_tick(0)
    frame_sums()
    partner_sums = exchange(pc, core, [partner], pcs, pcr)
    partner_sums[0].start()
    x_pass(0)
    x_start(1)
    y_tick(1)
    partner_sums[0].wait_recv()
    pz[z] = add_up(pc, 2)
    z_sums = exchange(pz, z, z_peers, pzs, pzr)
    for copy in z_sums:
        copy.start()
    for e in range(2):
        x_copy(1 - e, e, 0).wait_recv()
    y_tick(2)
    for copy in z_sums:
        copy.wait_recv()
    rsum[tcol] = scales(add_up(pz, 8))
    x_sums = exchange(rsum, tcol, x_peers, rss, rsr)
    for copy in x_sums:
        copy.start()
    for e in range(2):
        x2_copy(e, 0).wait_recv()
    y_tick(3)
    for copy in x_sums:
        copy.wait_recv()
    y_sums = [remote(rsum, csum, css.at[i], csr.at[i], peer) for i, peer in enumerate(y_peers)]

    @pl.when(offset == 0)
    def _():
        for copy in y_sums:
            copy.start()

    for block in range(4):
        tall = jnp.transpose(jnp.concatenate([rsum[block], jnp.zeros((120, local), jnp.float32)], axis=0))
        for e, h in pieces:
            rq[h, (2 * block + e) * sub : (2 * block + e + 1) * sub, :] = tall[(2 * e + h) * sub : (2 * e + h + 1) * sub]
    x_pass(1)
    y_tick(4)
    for i in range(3):
        @pl.when(offset == i + 1)
        def _():
            y_sums[i].wait_recv()

    for o in range(4):
        cq[o] = jnp.where(offset == 0, rsum[block_of(o)], csum[block_of(o)])
    y_arrived(0, 2)
    multiply(0)
    for e in range(2):
        x_copy(1 - e, e, 1).wait_recv()
    y_tick(5)
    advance(0, 1)
    for e in range(2):
        x2_copy(e, 1).wait_recv()
    y_tick(6)
    multiply(1)
    advance(0, 2)
    y_tick(7)
    advance(1, 1)
    advance(0, 3)
    advance(1, 2)
    y_tick(8)
    advance(0, 4)
    advance(1, 3)
    y_arrived(2, 6)
    for i in (2, 3):
        multiply(i)
    advance(0, 5)
    advance(1, 4)
    y_tick(9)
    for i in (4, 5):
        multiply(i)
    done = [5, 4, 0, 0, 0, 0, 0, 0]
    live = [0, 1, 2, 3, 4, 5]
    rounds = 0
    while min(done) < 7:
        for i in live:
            if done[i] < 7:
                done[i] += 1
                advance(i, done[i])
        rounds += 1
        if rounds == 1:
            y_arrived(6, 8)
            for i in (6, 7):
                multiply(i)
            live = list(range(8))

    for i, (h, o) in enumerate(STREAMS):
        @pl.when(core != h)
        def _():
            remote(handed.at[i], out_place(o, core), os_.at[i], or_.at[o], partner).wait_send()

        @pl.when(core == h)
        def _():
            pltpu.make_async_copy(handed.at[i], out_place(o, core), os_.at[i]).wait()
            remote(handed.at[i], out_place(o, 1 - core), os_.at[i], or_.at[o], partner).wait_recv()

    for e, h in pieces:
        give_copy(e, h).wait_send()
        x_copy(0, e, h).wait_send()
        x_copy(1, e, h).wait_send()
        x2_copy(e, h).wait_send()
    for d in range(2):
        @pl.when(position[d] < 3)
        def _():
            for i in range(8):
                y_next(d, i).wait_send()

    for copy in [*partner_sums, *z_sums, *x_sums]:
        copy.wait_send()

    @pl.when(offset == 0)
    def _():
        for copy in y_sums:
            copy.wait_send()

    def sent(step, carry):
        for i in range(8):
            remote(ring.at[i, step], ring.at[i, step], zs.at[i, step], zr.at[i, step], onward).wait_send()
        return carry

    lax.fori_loop(0, 7, sent, 0)


def per_device(frames, drift):
    local, _, tile_rows, columns = frames.shape
    total_frames = local * lax.axis_size("trow") * lax.axis_size("tcol")
    band_pixels = tile_rows * columns * lax.axis_size("pix")
    plain = frames.astype(jnp.bfloat16).transpose(1, 2, 0, 3)
    up = jnp.maximum(drift, 0).astype(jnp.float32) / 8.0
    down = jnp.maximum(-drift, 0).astype(jnp.float32) / 8.0
    stay = 1.0 - up - down
    weights = jnp.stack([stay[:, 0], up[:, 0], down[:, 0], stay[:, 1], up[:, 1], down[:, 1]], axis=1)

    dma = pltpu.SemaphoreType.DMA
    vmem = pl.BlockSpec(memory_space=pltpu.VMEM)
    block, half, sub = 4 * local, tile_rows * columns, local // 4
    f32, bf16, i16 = jnp.float32, jnp.bfloat16, jnp.int16
    out = pl.pallas_call(
        functools.partial(twotime_kernel, frames=float(total_frames), pixels=float(band_pixels)),
        out_shape=jax.ShapeDtypeStruct((2, block // 16, block), jnp.float32),
        in_specs=[vmem, vmem],
        out_specs=vmem,
        scratch_shapes=[
            pltpu.VMEM((2, 2, local, columns), bf16),
            pltpu.VMEM((2, tile_rows, local, columns), f32),
            pltpu.VMEM((2, 2, sub, half), bf16),
            pltpu.VMEM((2, block // 2, 2 * half), bf16),
            pltpu.VMEM((block, 2 * half), bf16),
            pltpu.VMEM((8, block // 2, local), i16),
            pltpu.VMEM((8, 7, sub, local), i16),
            pltpu.VMEM((8, sub, local), f32),
            pltpu.VMEM((4, 8, columns), f32),
            pltpu.VMEM((4, 8, columns), f32),
            pltpu.VMEM((2, 8, local), f32),
            pltpu.VMEM((8, 8, local), f32),
            pltpu.VMEM((4, 8, local), f32),
            pltpu.VMEM((4, 8, local), f32),
            pltpu.VMEM((2, block // 2, 128), f32),
            pltpu.VMEM((4, 8, local), f32),
            dma((2,)), dma((2,)), dma((3,)), dma((3,)), dma((3,)), dma((3,)), dma((2, 2)), dma((2, 2)),
            dma((2, 2, 2)), dma((2, 2, 2)), dma((2, 2)), dma((2, 2)), dma((2, 8)), dma((2, 8)), dma((2, 8)),
            dma((1,)), dma((1,)), dma((7,)), dma((7,)), dma((3,)), dma((3,)), dma((3,)), dma((3,)),
            dma((8, 7)), dma((8, 7)), dma((8,)), dma((4,)),
        ],
        compiler_params=pltpu.CompilerParams(collective_id=0, has_side_effects=True, vmem_limit_bytes=48 << 20),
        name="twotime",
    )(plain, weights)
    return out[0], out[1]


def solution(mesh):
    in_specs = (P(("trow", "tcol"), None, "pix", None), P(("trow", "tcol"), None))
    out_specs = (P(("trow", "pix"), "tcol"), P(("trow", "pix"), "tcol"))
    return jax.shard_map(
        per_device, mesh=mesh, in_specs=in_specs, out_specs=out_specs, check_vma=False
    )
```

```python
import functools

import jax
import jax.numpy as jnp
from jax import lax
from jax.experimental import pallas as pl
from jax.experimental.pallas import tpu as pltpu
from jax.sharding import PartitionSpec as P

MESH = pl.DeviceIdType.MESH
SCALE = 32000.0
OWN, WEST, EAST, FAR = range(4)
PATHS = tuple(
    tuple((o, band) for band in range(2) for o in blocks)
    for blocks in ((OWN, WEST, EAST, FAR), (OWN, EAST, WEST, FAR))
)
STREAMS = [(band, o) for band in range(2) for o in (OWN, WEST, EAST, FAR)]


def remote(src, dst, send, recv, device):
    return pltpu.make_async_remote_copy(
        src_ref=src, dst_ref=dst, send_sem=send, recv_sem=recv, device_id=device, device_id_type=MESH
    )


def around(index, step, count):
    return lax.rem(index + step + count, count)


def plan(tick, take_sums, y_arrived, multiply, start, advance):
    beat, hop, wire = 5.0, 2.5, 1.5
    todo = [(beat * t, 0, lambda t=t: tick(t)) for t in range(10)]
    ready = [beat * t for t in (4.4, 5.6, 5.7, 6.8, 7.6, 9.5, 9.6, 10.7)]
    clock, free, events = 0.0, 0.0, []
    for i, when in enumerate(ready):
        heads = [lambda: None]
        if i == 0:
            heads = [take_sums, lambda: y_arrived(0, 1)]
        elif i in (1, 3, 5, 7):
            heads = [lambda i=i: y_arrived(*((1, 3), (3, 4), (5, 7), (7, 8))[i // 2])]
        elif i == 4:
            heads = [lambda: y_arrived(4, 5)]
        for head in heads:
            todo.append((when, 1, head))
        todo.append((when, 2, lambda i=i: multiply(i)))
        events.append((when + 2.5, i, 0))
    while events:
        events.sort()
        when, i, step = events.pop(0)
        clock = max(clock + 0.3, when)
        todo.append((clock, 3, (lambda i=i: start(i)) if step == 0 else (lambda i=i, step=step: advance(i, step))))
        if step < 4:
            free = max(free, clock) + wire
            events.append((free + hop, i, step + 1))
    return [run for _, _, run in sorted(todo, key=lambda item: item[:2])]


def twotime_kernel(
    x_ref, w_ref, o_ref,
    halo, s, rows, cols, gram, mate, ring, px, py, pc, pz, rsum, csum, rq, cq,
    hs, hr, pxs, pxr, pys, pyr, ms, mr, xs, xr, x2s, x2r, ys, yr, yl,
    pcs, pcr, pzs, pzr, rss, rsr, css, csr, zs, zr,
    *, frames, pixels,
):
    trow, tcol, pix = lax.axis_index("trow"), lax.axis_index("tcol"), lax.axis_index("pix")
    z, core = pix // 2, lax.rem(pix, 2)
    way = 1 - 2 * core
    local = x_ref.shape[2]
    sub = local // 4
    half = 4 * 128
    x_peers = [{"tcol": around(tcol, i, 4)} for i in (1, 2, 3)]
    y_peers = [{"trow": around(trow, i, 4)} for i in (1, 2, 3)]
    z_peers = [{"pix": around(pix, 2 * i, 16)} for i in range(1, 8)]
    east, west = x_peers[0], x_peers[2]
    south, north = y_peers[0], y_peers[2]
    onward, backward = {"pix": around(pix, 2 * way, 16)}, {"pix": around(pix, -2 * way, 16)}
    partner = {"pix": pix + way}
    other = {"pix": around(pix, -way, 16)}
    above, below = {"pix": around(pix, -1, 16)}, {"pix": around(pix, 1, 16)}

    barrier = pltpu.get_barrier_semaphore()
    for device in [*x_peers, *y_peers, *z_peers, partner, other]:
        pl.semaphore_signal(barrier, inc=1, device_id=device, device_id_type=MESH)
    pl.semaphore_wait(barrier, 15)

    edges = [
        remote(x_ref.at[:, 3], halo.at[0], hs.at[0], hr.at[0], below),
        remote(x_ref.at[:, 0], halo.at[1], hs.at[1], hr.at[1], above),
    ]
    for copy in edges:
        copy.start()
    lane = lax.broadcasted_iota(jnp.int32, (sub, 128), 1)
    has_above = (pix > 0).astype(jnp.float32)
    has_below = (pix < 15).astype(jnp.float32)
    sums = [[jnp.zeros((8, 128), jnp.float32) for _ in range(4)] for _ in range(2)]
    for inner in (True, False):
        if not inner:
            for copy in edges:
                copy.wait()
        for t in range(4):
            at = pl.ds(t * sub, sub)
            stay_r, up_r, down_r, stay_c, up_c, down_c = (w_ref[at, i : i + 1] for i in range(6))
            up_c = jnp.where(lane < 127, up_c, 0.0)
            down_c = jnp.where(lane > 0, down_c, 0.0)
            for band in range(2):
                line = {r + 1: x_ref[band, r, at, :].astype(jnp.float32) for r in range(4)}
                if not inner:
                    line[0] = halo[0, band, at, :].astype(jnp.float32) * has_above
                    line[5] = halo[1, band, at, :].astype(jnp.float32) * has_below
                for r in (1, 2) if inner else (0, 3):
                    mid = stay_r * line[r + 1] + up_r * line[r + 2] + down_r * line[r]
                    moved = stay_c * mid + up_c * pltpu.roll(mid, 127, 1) + down_c * pltpu.roll(mid, 1, 1)
                    s[band, r, at, :] = moved
                    sums[band][r] += jnp.sum(moved.reshape(sub // 8, 8, 128), axis=0)
    for band in range(2):
        for r in range(4):
            px[tcol, 4 * band + r] = jnp.sum(sums[band][r], axis=0)

    def exchange(slots, own, peers, send, recv):
        return [remote(slots.at[own], slots.at[own], send.at[i], recv.at[i], peer) for i, peer in enumerate(peers)]

    def add_up(slots, count):
        total = slots[0]
        for i in range(1, count):
            total = total + slots[i]
        return total

    def meet(slots, own, peers, send, recv):
        copies = exchange(slots, own, peers, send, recv)
        for copy in copies:
            copy.start()
        for copy in copies:
            copy.wait()
        return add_up(slots, len(peers) + 1)

    py[trow] = meet(px, tcol, x_peers, pxs, pxr)
    px[tcol] = frames / meet(py, trow, y_peers, pys, pyr)

    def gain(band, r):
        return px[tcol, pl.ds(4 * band + r, 1), :]

    def part_of(block, e):
        return 2 * block + e

    def flatten(band):
        for e in range(2):
            for h in range(2):
                at = pl.ds((2 * e + h) * sub, sub)
                for r in range(4):
                    flat = s[band, r, at, :] * gain(band, r)
                    rows[band, part_of(tcol, e), h, :, r * 128 : (r + 1) * 128] = flat.astype(jnp.bfloat16)

    def x_copy(d, e, band):
        place = rows.at[band, part_of(tcol, e)]
        return remote(place, place, xs.at[d, e, band], xr.at[d, e, band], (east, west)[d])

    def x2_copy(e, band):
        place = rows.at[band, part_of(around(tcol, (-1, 1)[e], 4), e)]
        return remote(place, place, x2s.at[e, band], x2r.at[e, band], (east, west)[e])

    offset = around(trow, -tcol, 4)
    position = (offset, around(0, -offset, 4))

    def block_of(o):
        return around(tcol, (0, -1, 1, 2)[o], 4)

    def y_copies(d, i):
        o, band = PATHS[d][i]
        here, there = rows.at[band, part_of(block_of(o), d)], cols.at[band, part_of(block_of(o), d)]
        device = (south, north)[d]
        return here, there, device, ys.at[d, i], yr.at[d, i]

    def y_next(d, i):
        _, there, device, send, recv = y_copies(d, i)
        return remote(there, there, send, recv, device)

    def y_stay(d, i):
        here, there, _, _, _ = y_copies(d, i)
        return pltpu.make_async_copy(here, there, yl.at[d, i])

    def y_tick(tick):
        if tick < 8:
            @pl.when(offset == 0)
            def _():
                for d in range(2):
                    here, there, device, send, recv = y_copies(d, tick)
                    remote(here, there, send, recv, device).start()
                    y_stay(d, tick).start()

        for far in (1, 2):
            if 0 <= tick - far < 8:
                for d in range(2):
                    @pl.when(position[d] == far)
                    def _():
                        y_next(d, tick - far).wait_recv()
                        y_next(d, tick - far).start()

    def y_arrived(first, last):
        for i in range(first, last):
            for d in range(2):
                @pl.when(position[d] == 3)
                def _():
                    y_next(d, i).wait_recv()

                @pl.when(position[d] == 0)
                def _():
                    y_stay(d, i).wait()

    def x_start(h):
        x_copy(0, 0, h).start()
        x_copy(1, 1, h).start()
        x_copy(0, 1, h).start()
        x_copy(1, 0, h).start()

    def x_pass(h):
        for e in range(2):
            x_copy(e, e, h).wait_recv()
            x2_copy(e, h).start()

    chains = ((way, 4, 0, onward), (-way, 3, 4, backward))

    def toward(step, turn):
        return lax.rem(z + turn * step + 16, 8)

    def mate_copy(i):
        return remote(gram.at[i, 1 - core], mate.at[i], ms.at[i], mr.at[i], partner)

    def multiply(i):
        band, o = STREAMS[i]
        count = 2

        def product(h):
            def step(t, carry):
                at = pl.ds(pl.multiple_of(t * (8 // count), 8 // count), 8 // count)
                right = cols[band, pl.ds(part_of(block_of(o), 0), 2)].reshape(local, half)
                left = rows[band, at, h].reshape(8 // count * sub, half)
                value = lax.dot_general(left, right, (((1,), (1,)), ((), ())), preferred_element_type=jnp.float32)
                scale = rq[at, h, :, 2 * band : 2 * band + 1].reshape(8 // count * sub, 1)
                value = value * scale * cq[o, 2 * band : 2 * band + 1]
                value = jnp.round(value).astype(jnp.int32).astype(jnp.int16)
                gram[i, h, at] = value.reshape(8 // count, sub, local)
                return carry

            lax.fori_loop(0, count, step, 0)

        product(1 - core)
        mate_copy(i).start()
        product(core)

    def start(i):
        mate_copy(i).wait_recv()
        for c, (turn, length, first, device) in enumerate(chains):
            ring[i, 7 + c] = own(i, toward(length, turn)).astype(jnp.int16)
            remote(ring.at[i, 7 + c], ring.at[i, first], zs.at[i, first], zr.at[i, first], device).start()

    def z_arrived(i, k):
        remote(ring.at[i, k], ring.at[i, k], zs.at[i, k], zr.at[i, k], onward).wait_recv()

    def own(i, d):
        return gram[i, core, d].astype(jnp.int32) + mate[i, d].astype(jnp.int32)

    def advance(i, step):
        band, o = STREAMS[i]
        for turn, length, first, device in chains:
            if step < length:
                k = first + step
                z_arrived(i, k - 1)
                total = ring[i, k - 1].astype(jnp.int32) + own(i, toward(length - step, turn))
                ring[i, k - 1] = total.astype(jnp.int16)
                remote(ring.at[i, k - 1], ring.at[i, k], zs.at[i, k], zr.at[i, k], device).start()
        if step < 4:
            return
        z_arrived(i, 3)
        z_arrived(i, 6)
        final = ring[i, 3].astype(jnp.int32) + ring[i, 6].astype(jnp.int32) + own(i, z)
        final = final.astype(jnp.float32)
        final = final * rq[z, core, :, 2 * band + 1 : 2 * band + 2] * cq[o, 2 * band + 1 : 2 * band + 2]
        o_ref[band, :, pl.ds(pl.multiple_of(block_of(o) * local, local), local)] = final

    def frame_sums():
        wide = lax.broadcasted_iota(jnp.int32, (sub, 128), 1)
        for t in range(4):
            at = pl.ds(t * sub, sub)
            columns = jnp.zeros((sub, 128), jnp.float32)
            for band in range(2):
                plain = jnp.zeros((sub, 128), jnp.float32)
                square = jnp.zeros((sub, 128), jnp.float32)
                for r in range(4):
                    flat = s[band, r, at, :] * gain(band, r)
                    plain = plain + flat
                    square = square + flat * flat
                columns = jnp.where(wide == 2 * band, jnp.sum(plain, axis=1, keepdims=True), columns)
                columns = jnp.where(wide == 2 * band + 1, jnp.sum(square, axis=1, keepdims=True), columns)
            s[0, 0, at, :] = columns
        pc[core] = jnp.transpose(s[0, 0])[:8]

    def scales(total):
        result = []
        for band in range(2):
            norm = jnp.sqrt(total[2 * band + 1 : 2 * band + 2])
            result += [(SCALE**0.5) / norm, norm * (pixels / (SCALE * pixels) ** 0.5) / total[2 * band : 2 * band + 1]]
        return jnp.concatenate([*result, jnp.zeros((4, local), jnp.float32)], axis=0)

    partner_sums = exchange(pc, core, [partner], pcs, pcr)
    z_sums = exchange(pz, z, z_peers, pzs, pzr)
    x_sums = exchange(rsum, tcol, x_peers, rss, rsr)
    y_sums = [remote(rsum, csum, css.at[i], csr.at[i], peer) for i, peer in enumerate(y_peers)]

    def tick(t):
        if t == 0:
            flatten(0)
            x_start(0)
        if t in (1, 4):
            x_pass(t // 4)
        if t in (2, 5):
            for e in range(2):
                x_copy(1 - e, e, t // 4).wait_recv()
        if t in (3, 6):
            for e in range(2):
                x2_copy(e, t // 4).wait_recv()
        y_tick(t)
        if t == 0:
            frame_sums()
            partner_sums[0].start()
            flatten(1)
            partner_sums[0].wait_recv()
            pz[z] = add_up(pc, 2)
            for copy in z_sums:
                copy.start()
        if t == 1:
            for copy in z_sums:
                copy.wait_recv()
            rsum[tcol] = scales(add_up(pz, 8))
            for copy in x_sums:
                copy.start()
            x_start(1)
        if t == 2:
            for copy in x_sums:
                copy.wait_recv()

            @pl.when(offset == 0)
            def _():
                for copy in y_sums:
                    copy.start()

            for block in range(4):
                tall = jnp.transpose(jnp.concatenate([rsum[block], jnp.zeros((120, local), jnp.float32)], axis=0))
                rq[2 * block : 2 * block + 2] = tall.reshape(2, 2, sub, 128)

    def take_sums():
        for i in range(3):
            @pl.when(offset == i + 1)
            def _():
                y_sums[i].wait_recv()

        for o in range(4):
            cq[o] = jnp.where(offset == 0, rsum[block_of(o)], csum[block_of(o)])

    for run in plan(tick, take_sums, y_arrived, multiply, start, advance):
        run()

    for i in range(8):
        mate_copy(i).wait_send()
    for band in range(2):
        for e in range(2):
            x_copy(0, e, band).wait_send()
            x_copy(1, e, band).wait_send()
            x2_copy(e, band).wait_send()
    for d in range(2):
        @pl.when(position[d] < 3)
        def _():
            for i in range(8):
                y_next(d, i).wait_send()

    for copy in [*partner_sums, *z_sums, *x_sums]:
        copy.wait_send()

    @pl.when(offset == 0)
    def _():
        for copy in y_sums:
            copy.wait_send()

    def sent(step, carry):
        for i in range(8):
            remote(ring.at[i, step], ring.at[i, step], zs.at[i, step], zr.at[i, step], onward).wait_send()
        return carry

    lax.fori_loop(0, 7, sent, 0)


def per_device(frames, drift):
    local, _, tile_rows, columns = frames.shape
    total_frames = local * lax.axis_size("trow") * lax.axis_size("tcol")
    band_pixels = tile_rows * columns * lax.axis_size("pix")
    plain = frames.astype(jnp.bfloat16).transpose(1, 2, 0, 3)
    up = jnp.maximum(drift, 0).astype(jnp.float32) / 8.0
    down = jnp.maximum(-drift, 0).astype(jnp.float32) / 8.0
    stay = 1.0 - up - down
    weights = jnp.stack([stay[:, 0], up[:, 0], down[:, 0], stay[:, 1], up[:, 1], down[:, 1]], axis=1)

    dma = pltpu.SemaphoreType.DMA
    vmem = pl.BlockSpec(memory_space=pltpu.VMEM)
    block, half, sub = 4 * local, tile_rows * columns, local // 4
    f32, bf16, i16 = jnp.float32, jnp.bfloat16, jnp.int16
    out = pl.pallas_call(
        functools.partial(twotime_kernel, frames=float(total_frames), pixels=float(band_pixels)),
        out_shape=jax.ShapeDtypeStruct((2, block // 16, block), jnp.float32),
        in_specs=[vmem, vmem],
        out_specs=vmem,
        scratch_shapes=[
            pltpu.VMEM((2, 2, local, columns), bf16),
            pltpu.VMEM((2, tile_rows, local, columns), f32),
            pltpu.VMEM((2, 8, 2, sub, half), bf16),
            pltpu.VMEM((2, 8, 2, sub, half), bf16),
            pltpu.VMEM((8, 2, 8, sub, local), i16),
            pltpu.VMEM((8, 8, sub, local), i16),
            pltpu.VMEM((8, 9, sub, local), i16),
            pltpu.VMEM((4, 8, columns), f32),
            pltpu.VMEM((4, 8, columns), f32),
            pltpu.VMEM((2, 8, local), f32),
            pltpu.VMEM((8, 8, local), f32),
            pltpu.VMEM((4, 8, local), f32),
            pltpu.VMEM((4, 8, local), f32),
            pltpu.VMEM((8, 2, sub, 128), f32),
            pltpu.VMEM((4, 8, local), f32),
            dma((2,)), dma((2,)), dma((3,)), dma((3,)), dma((3,)), dma((3,)), dma((8,)), dma((8,)),
            dma((2, 2, 2)), dma((2, 2, 2)), dma((2, 2)), dma((2, 2)), dma((2, 8)), dma((2, 8)), dma((2, 8)),
            dma((1,)), dma((1,)), dma((7,)), dma((7,)), dma((3,)), dma((3,)), dma((3,)), dma((3,)),
            dma((8, 7)), dma((8, 7)),
        ],
        compiler_params=pltpu.CompilerParams(collective_id=0, has_side_effects=True, vmem_limit_bytes=48 << 20),
        name="twotime",
    )(plain, weights)
    return out[0], out[1]


def solution(mesh):
    in_specs = (P(("trow", "tcol"), None, "pix", None), P(("trow", "tcol"), None))
    out_specs = (P(("trow", "pix"), "tcol"), P(("trow", "pix"), "tcol"))
    return jax.shard_map(
        per_device, mesh=mesh, in_specs=in_specs, out_specs=out_specs, check_vma=False
    )
```

```python
import functools

import jax
import jax.numpy as jnp
from jax import lax
from jax.experimental import pallas as pl
from jax.experimental.pallas import tpu as pltpu
from jax.sharding import PartitionSpec as P

MESH = pl.DeviceIdType.MESH
SCALE = 32000.0
OWN, WEST, EAST, FAR = range(4)
PATHS = tuple(
    tuple((o, band) for band in range(2) for o in blocks)
    for blocks in ((OWN, WEST, EAST, FAR), (OWN, EAST, WEST, FAR))
)
STREAMS = [(band, o) for band in range(2) for o in (OWN, WEST, EAST, FAR)]


def remote(src, dst, send, recv, device):
    return pltpu.make_async_remote_copy(
        src_ref=src, dst_ref=dst, send_sem=send, recv_sem=recv, device_id=device, device_id_type=MESH
    )


def around(index, step, count):
    return lax.rem(index + step + count, count)


def plan(tick, take_sums, y_arrived, multiply, start, advance):
    beat, hop, wire = 4.5, 3.0, 1.5
    todo = [(beat * t, 0, lambda t=t: tick(t)) for t in range(10)]
    ready = [beat * t for t in (4.4, 5.6, 5.7, 6.8, 7.6, 9.5, 9.6, 10.7)]
    clock, free, events = 0.0, 0.0, []
    for i, when in enumerate(ready):
        heads = [lambda: None]
        if i == 0:
            heads = [take_sums, lambda: y_arrived(0, 1)]
        elif i in (1, 3, 5, 7):
            heads = [lambda i=i: y_arrived(*((1, 3), (3, 4), (5, 7), (7, 8))[i // 2])]
        elif i == 4:
            heads = [lambda: y_arrived(4, 5)]
        for head in heads:
            todo.append((when, 1, head))
        todo.append((when, 2, lambda i=i: multiply(i)))
        events.append((when + 2.5, i, 0))
    while events:
        events.sort()
        when, i, step = events.pop(0)
        clock = max(clock + 0.3, when)
        todo.append((clock, 3, (lambda i=i: start(i)) if step == 0 else (lambda i=i, step=step: advance(i, step))))
        if step < 4:
            free = max(free, clock) + wire
            events.append((free + hop, i, step + 1))
    return [run for _, _, run in sorted(todo, key=lambda item: item[:2])]


def twotime_kernel(
    x_ref, w_ref, o_ref,
    halo, s, rows, cols, gram, mate, ring, px, py, pc, pz, rsum, csum, rq, cq,
    hs, hr, pxs, pxr, pys, pyr, ms, mr, xs, xr, x2s, x2r, ys, yr, yl,
    pcs, pcr, pzs, pzr, rss, rsr, css, csr, zs, zr,
    *, frames, pixels,
):
    trow, tcol, pix = lax.axis_index("trow"), lax.axis_index("tcol"), lax.axis_index("pix")
    z, core = pix // 2, lax.rem(pix, 2)
    way = 1 - 2 * core
    local = x_ref.shape[2]
    sub = local // 4
    half = 4 * 128
    x_peers = [{"tcol": around(tcol, i, 4)} for i in (1, 2, 3)]
    y_peers = [{"trow": around(trow, i, 4)} for i in (1, 2, 3)]
    z_peers = [{"pix": around(pix, 2 * i, 16)} for i in range(1, 8)]
    east, west = x_peers[0], x_peers[2]
    south, north = y_peers[0], y_peers[2]
    onward, backward = {"pix": around(pix, 2 * way, 16)}, {"pix": around(pix, -2 * way, 16)}
    partner = {"pix": pix + way}
    other = {"pix": around(pix, -way, 16)}
    above, below = {"pix": around(pix, -1, 16)}, {"pix": around(pix, 1, 16)}

    barrier = pltpu.get_barrier_semaphore()
    for device in [*x_peers, *y_peers, *z_peers, partner, other]:
        pl.semaphore_signal(barrier, inc=1, device_id=device, device_id_type=MESH)
    pl.semaphore_wait(barrier, 15)

    edges = [
        remote(x_ref.at[:, 3], halo.at[0], hs.at[0], hr.at[0], below),
        remote(x_ref.at[:, 0], halo.at[1], hs.at[1], hr.at[1], above),
    ]
    for copy in edges:
        copy.start()
    lane = lax.broadcasted_iota(jnp.int32, (sub, 128), 1)
    has_above = (pix > 0).astype(jnp.float32)
    has_below = (pix < 15).astype(jnp.float32)
    sums = [[jnp.zeros((8, 128), jnp.float32) for _ in range(4)] for _ in range(2)]
    for inner in (True, False):
        if not inner:
            for copy in edges:
                copy.wait()
        for t in range(4):
            at = pl.ds(t * sub, sub)
            stay_r, up_r, down_r, stay_c, up_c, down_c = (w_ref[at, i : i + 1] for i in range(6))
            up_c = jnp.where(lane < 127, up_c, 0.0)
            down_c = jnp.where(lane > 0, down_c, 0.0)
            for band in range(2):
                line = {r + 1: x_ref[band, r, at, :].astype(jnp.float32) for r in range(4)}
                if not inner:
                    line[0] = halo[0, band, at, :].astype(jnp.float32) * has_above
                    line[5] = halo[1, band, at, :].astype(jnp.float32) * has_below
                for r in (1, 2) if inner else (0, 3):
                    mid = stay_r * line[r + 1] + up_r * line[r + 2] + down_r * line[r]
                    moved = stay_c * mid + up_c * pltpu.roll(mid, 127, 1) + down_c * pltpu.roll(mid, 1, 1)
                    s[band, r, at, :] = moved
                    sums[band][r] += jnp.sum(moved.reshape(sub // 8, 8, 128), axis=0)
    for band in range(2):
        for r in range(4):
            px[tcol, 4 * band + r] = jnp.sum(sums[band][r], axis=0)

    def exchange(slots, own, peers, send, recv):
        return [remote(slots.at[own], slots.at[own], send.at[i], recv.at[i], peer) for i, peer in enumerate(peers)]

    def add_up(slots, count):
        total = slots[0]
        for i in range(1, count):
            total = total + slots[i]
        return total

    def meet(slots, own, peers, send, recv):
        copies = exchange(slots, own, peers, send, recv)
        for copy in copies:
            copy.start()
        for copy in copies:
            copy.wait()
        return add_up(slots, len(peers) + 1)

    py[trow] = meet(px, tcol, x_peers, pxs, pxr)
    px[tcol] = frames / meet(py, trow, y_peers, pys, pyr)

    def gain(band, r):
        return px[tcol, pl.ds(4 * band + r, 1), :]

    def part_of(block, e):
        return 2 * block + e

    def flatten(band):
        for e in range(2):
            for h in range(2):
                at = pl.ds((2 * e + h) * sub, sub)
                for r in range(4):
                    flat = s[band, r, at, :] * gain(band, r)
                    rows[band, part_of(tcol, e), h, :, r * 128 : (r + 1) * 128] = flat.astype(jnp.bfloat16)

    def x_copy(d, e, band, h):
        place = rows.at[band, part_of(tcol, e), h]
        return remote(place, place, xs.at[d, e, band, h], xr.at[d, e, band, h], (east, west)[d])

    def x2_copy(e, band, h):
        place = rows.at[band, part_of(around(tcol, (-1, 1)[e], 4), e), h]
        return remote(place, place, x2s.at[e, band, h], x2r.at[e, band, h], (east, west)[e])

    offset = around(trow, -tcol, 4)
    position = (offset, around(0, -offset, 4))

    def block_of(o):
        return around(tcol, (0, -1, 1, 2)[o], 4)

    def y_copies(d, i):
        o, band = PATHS[d][i]
        here, there = rows.at[band, part_of(block_of(o), d)], cols.at[band, part_of(block_of(o), d)]
        device = (south, north)[d]
        return here, there, device, ys.at[d, i], yr.at[d, i]

    def y_next(d, i, h):
        _, there, device, send, recv = y_copies(d, i)
        return remote(there.at[h], there.at[h], send.at[h], recv.at[h], device)

    def y_stay(d, i):
        here, there, _, _, _ = y_copies(d, i)
        return pltpu.make_async_copy(here, there, yl.at[d, i])

    def y_tick(tick):
        if tick < 8:
            @pl.when(offset == 0)
            def _():
                for h in range(2):
                    for d in range(2):
                        here, there, device, send, recv = y_copies(d, tick)
                        remote(here.at[h], there.at[h], send.at[h], recv.at[h], device).start()
                for d in range(2):
                    y_stay(d, tick).start()

        for far in (1, 2):
            if 0 <= tick - far < 8:
                for h in range(2):
                    for d in range(2):
                        @pl.when(position[d] == far)
                        def _():
                            y_next(d, tick - far, h).wait_recv()
                            y_next(d, tick - far, h).start()

    def y_arrived(first, last):
        for i in range(first, last):
            for d in range(2):
                @pl.when(position[d] == 3)
                def _():
                    for h in range(2):
                        y_next(d, i, h).wait_recv()

                @pl.when(position[d] == 0)
                def _():
                    y_stay(d, i).wait()

    def x_start(band, step):
        for h in range(2):
            for d in range(2):
                x_copy(d, (d + step) % 2, band, h).start()

    def x_pass(band):
        for h in range(2):
            for e in range(2):
                x_copy(e, e, band, h).wait_recv()
                x2_copy(e, band, h).start()

    chains = ((way, 4, 0, onward), (-way, 3, 4, backward))

    def toward(step, turn):
        return lax.rem(z + turn * step + 16, 8)

    def mate_copy(i):
        return remote(gram.at[i, 1 - core], mate.at[i], ms.at[i], mr.at[i], partner)

    def multiply(i):
        band, o = STREAMS[i]
        count = 2

        def product(h):
            def step(t, carry):
                at = pl.ds(pl.multiple_of(t * (8 // count), 8 // count), 8 // count)
                right = cols[band, pl.ds(part_of(block_of(o), 0), 2)].reshape(local, half)
                left = rows[band, at, h].reshape(8 // count * sub, half)
                value = lax.dot_general(left, right, (((1,), (1,)), ((), ())), preferred_element_type=jnp.float32)
                scale = rq[at, h, :, 2 * band : 2 * band + 1].reshape(8 // count * sub, 1)
                value = value * scale * cq[o, 2 * band : 2 * band + 1]
                value = jnp.round(value).astype(jnp.int32).astype(jnp.int16)
                gram[i, h, at] = value.reshape(8 // count, sub, local)
                return carry

            lax.fori_loop(0, count, step, 0)

        product(1 - core)
        mate_copy(i).start()
        product(core)

    def start(i):
        mate_copy(i).wait_recv()
        for c, (turn, length, first, device) in enumerate(chains):
            ring[i, 7 + c] = own(i, toward(length, turn)).astype(jnp.int16)
            remote(ring.at[i, 7 + c], ring.at[i, first], zs.at[i, first], zr.at[i, first], device).start()

    def z_arrived(i, k):
        remote(ring.at[i, k], ring.at[i, k], zs.at[i, k], zr.at[i, k], onward).wait_recv()

    def own(i, d):
        return gram[i, core, d].astype(jnp.int32) + mate[i, d].astype(jnp.int32)

    def advance(i, step):
        band, o = STREAMS[i]
        for turn, length, first, device in chains:
            if step < length:
                k = first + step
                z_arrived(i, k - 1)
                total = ring[i, k - 1].astype(jnp.int32) + own(i, toward(length - step, turn))
                ring[i, k - 1] = total.astype(jnp.int16)
                remote(ring.at[i, k - 1], ring.at[i, k], zs.at[i, k], zr.at[i, k], device).start()
        if step < 4:
            return
        z_arrived(i, 3)
        z_arrived(i, 6)
        final = ring[i, 3].astype(jnp.int32) + ring[i, 6].astype(jnp.int32) + own(i, z)
        final = final.astype(jnp.float32)
        final = final * rq[z, core, :, 2 * band + 1 : 2 * band + 2] * cq[o, 2 * band + 1 : 2 * band + 2]
        o_ref[band, :, pl.ds(pl.multiple_of(block_of(o) * local, local), local)] = final

    def frame_sums():
        wide = lax.broadcasted_iota(jnp.int32, (sub, 128), 1)
        for t in range(4):
            at = pl.ds(t * sub, sub)
            columns = jnp.zeros((sub, 128), jnp.float32)
            for band in range(2):
                plain = jnp.zeros((sub, 128), jnp.float32)
                square = jnp.zeros((sub, 128), jnp.float32)
                for r in range(4):
                    flat = s[band, r, at, :] * gain(band, r)
                    plain = plain + flat
                    square = square + flat * flat
                columns = jnp.where(wide == 2 * band, jnp.sum(plain, axis=1, keepdims=True), columns)
                columns = jnp.where(wide == 2 * band + 1, jnp.sum(square, axis=1, keepdims=True), columns)
            s[0, 0, at, :] = columns
        pc[core] = jnp.transpose(s[0, 0])[:8]

    def scales(total):
        result = []
        for band in range(2):
            norm = jnp.sqrt(total[2 * band + 1 : 2 * band + 2])
            result += [(SCALE**0.5) / norm, norm * (pixels / (SCALE * pixels) ** 0.5) / total[2 * band : 2 * band + 1]]
        return jnp.concatenate([*result, jnp.zeros((4, local), jnp.float32)], axis=0)

    partner_sums = exchange(pc, core, [partner], pcs, pcr)
    z_sums = exchange(pz, z, z_peers, pzs, pzr)
    x_sums = exchange(rsum, tcol, x_peers, rss, rsr)
    y_sums = [remote(rsum, csum, css.at[i], csr.at[i], peer) for i, peer in enumerate(y_peers)]

    def tick(t):
        if t == 0:
            flatten(0)
            x_start(0, 0)
        if t in (1, 4):
            x_pass(t // 4)
        if t in (2, 5):
            for e in range(2):
                for h in range(2):
                    x_copy(1 - e, e, t // 4, h).wait_recv()
        if t in (3, 6):
            for e in range(2):
                for h in range(2):
                    x2_copy(e, t // 4, h).wait_recv()
        y_tick(t)
        if t in (2, 3):
            x_start(1, t - 2)
        if t == 0:
            x_start(0, 1)
            frame_sums()
            partner_sums[0].start()
            flatten(1)
            partner_sums[0].wait_recv()
            pz[z] = add_up(pc, 2)
            for copy in z_sums:
                copy.start()
        if t == 1:
            for copy in z_sums:
                copy.wait_recv()
            rsum[tcol] = scales(add_up(pz, 8))
            for copy in x_sums:
                copy.start()
        if t == 3:
            for copy in x_sums:
                copy.wait_recv()

            @pl.when(offset == 0)
            def _():
                for copy in y_sums:
                    copy.start()

            for block in range(4):
                tall = jnp.transpose(jnp.concatenate([rsum[block], jnp.zeros((120, local), jnp.float32)], axis=0))
                rq[2 * block : 2 * block + 2] = tall.reshape(2, 2, sub, 128)

    def take_sums():
        for i in range(3):
            @pl.when(offset == i + 1)
            def _():
                y_sums[i].wait_recv()

        for o in range(4):
            cq[o] = jnp.where(offset == 0, rsum[block_of(o)], csum[block_of(o)])

    for run in plan(tick, take_sums, y_arrived, multiply, start, advance):
        run()

    for i in range(8):
        mate_copy(i).wait_send()
    for band in range(2):
        for e in range(2):
            for h in range(2):
                x_copy(0, e, band, h).wait_send()
                x_copy(1, e, band, h).wait_send()
                x2_copy(e, band, h).wait_send()
    for d in range(2):
        @pl.when(position[d] < 3)
        def _():
            for i in range(8):
                for h in range(2):
                    y_next(d, i, h).wait_send()

    for copy in [*partner_sums, *z_sums, *x_sums]:
        copy.wait_send()

    @pl.when(offset == 0)
    def _():
        for copy in y_sums:
            copy.wait_send()

    def sent(step, carry):
        for i in range(8):
            remote(ring.at[i, step], ring.at[i, step], zs.at[i, step], zr.at[i, step], onward).wait_send()
        return carry

    lax.fori_loop(0, 7, sent, 0)


def per_device(frames, drift):
    local, _, tile_rows, columns = frames.shape
    total_frames = local * lax.axis_size("trow") * lax.axis_size("tcol")
    band_pixels = tile_rows * columns * lax.axis_size("pix")
    plain = frames.astype(jnp.bfloat16).transpose(1, 2, 0, 3)
    up = jnp.maximum(drift, 0).astype(jnp.float32) / 8.0
    down = jnp.maximum(-drift, 0).astype(jnp.float32) / 8.0
    stay = 1.0 - up - down
    weights = jnp.stack([stay[:, 0], up[:, 0], down[:, 0], stay[:, 1], up[:, 1], down[:, 1]], axis=1)

    dma = pltpu.SemaphoreType.DMA
    vmem = pl.BlockSpec(memory_space=pltpu.VMEM)
    block, half, sub = 4 * local, tile_rows * columns, local // 4
    f32, bf16, i16 = jnp.float32, jnp.bfloat16, jnp.int16
    out = pl.pallas_call(
        functools.partial(twotime_kernel, frames=float(total_frames), pixels=float(band_pixels)),
        out_shape=jax.ShapeDtypeStruct((2, block // 16, block), jnp.float32),
        in_specs=[vmem, vmem],
        out_specs=vmem,
        scratch_shapes=[
            pltpu.VMEM((2, 2, local, columns), bf16),
            pltpu.VMEM((2, tile_rows, local, columns), f32),
            pltpu.VMEM((2, 8, 2, sub, half), bf16),
            pltpu.VMEM((2, 8, 2, sub, half), bf16),
            pltpu.VMEM((8, 2, 8, sub, local), i16),
            pltpu.VMEM((8, 8, sub, local), i16),
            pltpu.VMEM((8, 9, sub, local), i16),
            pltpu.VMEM((4, 8, columns), f32),
            pltpu.VMEM((4, 8, columns), f32),
            pltpu.VMEM((2, 8, local), f32),
            pltpu.VMEM((8, 8, local), f32),
            pltpu.VMEM((4, 8, local), f32),
            pltpu.VMEM((4, 8, local), f32),
            pltpu.VMEM((8, 2, sub, 128), f32),
            pltpu.VMEM((4, 8, local), f32),
            dma((2,)), dma((2,)), dma((3,)), dma((3,)), dma((3,)), dma((3,)), dma((8,)), dma((8,)),
            dma((2, 2, 2, 2)), dma((2, 2, 2, 2)), dma((2, 2, 2)), dma((2, 2, 2)), dma((2, 8, 2)), dma((2, 8, 2)), dma((2, 8)),
            dma((1,)), dma((1,)), dma((7,)), dma((7,)), dma((3,)), dma((3,)), dma((3,)), dma((3,)),
            dma((8, 7)), dma((8, 7)),
        ],
        compiler_params=pltpu.CompilerParams(collective_id=0, has_side_effects=True, vmem_limit_bytes=48 << 20),
        name="twotime",
    )(plain, weights)
    return out[0], out[1]


def solution(mesh):
    in_specs = (P(("trow", "tcol"), None, "pix", None), P(("trow", "tcol"), None))
    out_specs = (P(("trow", "pix"), "tcol"), P(("trow", "pix"), "tcol"))
    return jax.shard_map(
        per_device, mesh=mesh, in_specs=in_specs, out_specs=out_specs, check_vma=False
    )
```

```python
import functools

import jax
import jax.numpy as jnp
from jax import lax
from jax.experimental import pallas as pl
from jax.experimental.pallas import tpu as pltpu
from jax.sharding import PartitionSpec as P

MESH = pl.DeviceIdType.MESH
SCALE = 32000.0
OWN, WEST, EAST, FAR = range(4)
PATHS = tuple(
    tuple((o, band) for band in range(2) for o in blocks)
    for blocks in ((OWN, WEST, EAST, FAR), (OWN, EAST, WEST, FAR))
)
STREAMS = [(band, o) for band in range(2) for o in (OWN, WEST, EAST, FAR)]


def remote(src, dst, send, recv, device):
    return pltpu.make_async_remote_copy(
        src_ref=src, dst_ref=dst, send_sem=send, recv_sem=recv, device_id=device, device_id_type=MESH
    )


def around(index, step, count):
    return lax.rem(index + step + count, count)


def plan(tick, take_sums, y_arrived, multiply, start, advance):
    beat, hop, wire = 4.5, 3.0, 1.5
    todo = [(beat * t, 0, lambda t=t: tick(t)) for t in range(10)]
    ready = [beat * t for t in (4.4, 5.6, 5.7, 6.8, 7.6, 9.5, 9.6, 10.7)]
    clock, free, events = 0.0, 0.0, []
    for i, when in enumerate(ready):
        heads = [lambda: None]
        if i == 0:
            heads = [take_sums, lambda: y_arrived(0, 1)]
        elif i in (1, 3, 5, 7):
            heads = [lambda i=i: y_arrived(*((1, 3), (3, 4), (5, 7), (7, 8))[i // 2])]
        elif i == 4:
            heads = [lambda: y_arrived(4, 5)]
        for head in heads:
            todo.append((when, 1, head))
        todo.append((when, 2, lambda i=i: multiply(i)))
        events.append((when + 2.5, i, 0))
    while events:
        events.sort()
        when, i, step = events.pop(0)
        clock = max(clock + 0.3, when)
        todo.append((clock, 3, (lambda i=i: start(i)) if step == 0 else (lambda i=i, step=step: advance(i, step))))
        if step < 4:
            free = max(free, clock) + wire
            events.append((free + hop, i, step + 1))
    return [run for _, _, run in sorted(todo, key=lambda item: item[:2])]


def twotime_kernel(
    x_ref, w_ref, o_ref,
    halo, s, rows, cols, gram, mate, ring, px, py, pc, pz, rsum, csum, rq, cq,
    hs, hr, pxs, pxr, pys, pyr, ms, mr, xs, xr, x2s, x2r, ys, yr, yl, yd,
    pcs, pcr, pzs, pzr, rss, rsr, css, csr, zs, zr,
    *, frames, pixels,
):
    trow, tcol, pix = lax.axis_index("trow"), lax.axis_index("tcol"), lax.axis_index("pix")
    z, core = pix // 2, lax.rem(pix, 2)
    way = 1 - 2 * core
    local = x_ref.shape[2]
    sub = local // 4
    half = 4 * 128
    x_peers = [{"tcol": around(tcol, i, 4)} for i in (1, 2, 3)]
    y_peers = [{"trow": around(trow, i, 4)} for i in (1, 2, 3)]
    z_peers = [{"pix": around(pix, 2 * i, 16)} for i in range(1, 8)]
    east, west = x_peers[0], x_peers[2]
    south, north = y_peers[0], y_peers[2]
    onward, backward = {"pix": around(pix, 2 * way, 16)}, {"pix": around(pix, -2 * way, 16)}
    partner = {"pix": pix + way}
    other = {"pix": around(pix, -way, 16)}
    above, below = {"pix": around(pix, -1, 16)}, {"pix": around(pix, 1, 16)}

    barrier = pltpu.get_barrier_semaphore()
    for device in [*x_peers, *y_peers, *z_peers, partner, other]:
        pl.semaphore_signal(barrier, inc=1, device_id=device, device_id_type=MESH)
    pl.semaphore_wait(barrier, 15)

    edges = [
        remote(x_ref.at[:, 3], halo.at[0], hs.at[0], hr.at[0], below),
        remote(x_ref.at[:, 0], halo.at[1], hs.at[1], hr.at[1], above),
    ]
    for copy in edges:
        copy.start()
    lane = lax.broadcasted_iota(jnp.int32, (sub, 128), 1)
    has_above = (pix > 0).astype(jnp.float32)
    has_below = (pix < 15).astype(jnp.float32)
    sums = [[jnp.zeros((8, 128), jnp.float32) for _ in range(4)] for _ in range(2)]
    for inner in (True, False):
        if not inner:
            for copy in edges:
                copy.wait()
        for t in range(4):
            at = pl.ds(t * sub, sub)
            stay_r, up_r, down_r, stay_c, up_c, down_c = (w_ref[at, i : i + 1] for i in range(6))
            up_c = jnp.where(lane < 127, up_c, 0.0)
            down_c = jnp.where(lane > 0, down_c, 0.0)
            for band in range(2):
                line = {r + 1: x_ref[band, r, at, :].astype(jnp.float32) for r in range(4)}
                if not inner:
                    line[0] = halo[0, band, at, :].astype(jnp.float32) * has_above
                    line[5] = halo[1, band, at, :].astype(jnp.float32) * has_below
                for r in (1, 2) if inner else (0, 3):
                    mid = stay_r * line[r + 1] + up_r * line[r + 2] + down_r * line[r]
                    moved = stay_c * mid + up_c * pltpu.roll(mid, 127, 1) + down_c * pltpu.roll(mid, 1, 1)
                    s[band, r, at, :] = moved
                    sums[band][r] += jnp.sum(moved.reshape(sub // 8, 8, 128), axis=0)
    for band in range(2):
        for r in range(4):
            px[tcol, 4 * band + r] = jnp.sum(sums[band][r], axis=0)

    def exchange(slots, own, peers, send, recv):
        return [remote(slots.at[own], slots.at[own], send.at[i], recv.at[i], peer) for i, peer in enumerate(peers)]

    def add_up(slots, count):
        total = slots[0]
        for i in range(1, count):
            total = total + slots[i]
        return total

    def meet(slots, own, peers, send, recv):
        copies = exchange(slots, own, peers, send, recv)
        for copy in copies:
            copy.start()
        for copy in copies:
            copy.wait()
        return add_up(slots, len(peers) + 1)

    py[trow] = meet(px, tcol, x_peers, pxs, pxr)
    px[tcol] = frames / meet(py, trow, y_peers, pys, pyr)

    def gain(band, r):
        return px[tcol, pl.ds(4 * band + r, 1), :]

    def part_of(block, e):
        return 2 * block + e

    def flatten(band):
        for e in range(2):
            for h in range(2):
                at = pl.ds((2 * e + h) * sub, sub)
                for r in range(4):
                    flat = s[band, r, at, :] * gain(band, r)
                    rows[band, part_of(tcol, e), h, :, r * 128 : (r + 1) * 128] = flat.astype(jnp.bfloat16)

    def x_copy(d, e, band, h):
        place = rows.at[band, part_of(tcol, e), h]
        return remote(place, place, xs.at[d, e, band, h], xr.at[d, e, band, h], (east, west)[d])

    def x2_copy(e, band, h):
        place = rows.at[band, part_of(around(tcol, (-1, 1)[e], 4), e), h]
        return remote(place, place, x2s.at[e, band, h], x2r.at[e, band, h], (east, west)[e])

    offset = around(trow, -tcol, 4)
    position = (offset, around(0, -offset, 4))

    def block_of(o):
        return around(tcol, (0, -1, 1, 2)[o], 4)

    def y_copies(d, i):
        o, band = PATHS[d][i]
        here, there = rows.at[band, part_of(block_of(o), d)], cols.at[band, part_of(block_of(o), d)]
        device = (south, north)[d]
        return here, there, device, ys.at[d, i], yr.at[d, i]

    def y_next(d, i, h):
        _, there, device, send, recv = y_copies(d, i)
        return remote(there.at[h], there.at[h], send.at[h], recv.at[h], device)

    def y_stay(d, i):
        here, there, _, _, _ = y_copies(d, i)
        return pltpu.make_async_copy(here, there, yl.at[d, i])

    def y_direct(d, h):
        here, there, _, _, recv = y_copies(d, 7)
        return remote(here.at[h], there.at[h], yd.at[d, h], recv.at[h], (north, south)[d])

    def y_tick(tick):
        if tick < 8:
            @pl.when(offset == 0)
            def _():
                for h in range(2):
                    for d in range(2):
                        here, there, device, send, recv = y_copies(d, tick)
                        remote(here.at[h], there.at[h], send.at[h], recv.at[h], device).start()
                for d in range(2):
                    y_stay(d, tick).start()
                if tick == 7:
                    for d in range(2):
                        for h in range(2):
                            y_direct(d, h).start()

        for far in (1, 2):
            if 0 <= tick - far < 8:
                for h in range(2):
                    for d in range(2):
                        @pl.when(position[d] == far)
                        def _():
                            y_next(d, tick - far, h).wait_recv()
                            if (far, tick) != (2, 9):
                                y_next(d, tick - far, h).start()

    def y_arrived(first, last):
        for i in range(first, last):
            for d in range(2):
                @pl.when(position[d] == 3)
                def _():
                    for h in range(2):
                        y_next(d, i, h).wait_recv()

                @pl.when(position[d] == 0)
                def _():
                    y_stay(d, i).wait()

    def x_start(band, step):
        for h in range(2):
            for d in range(2):
                x_copy(d, (d + step) % 2, band, h).start()

    def x_pass(band):
        for h in range(2):
            for e in range(2):
                x_copy(e, e, band, h).wait_recv()
                x2_copy(e, band, h).start()

    chains = ((way, 4, 0, onward), (-way, 3, 4, backward))

    def toward(step, turn):
        return lax.rem(z + turn * step + 16, 8)

    def mate_copy(i):
        return remote(gram.at[i, 1 - core], mate.at[i], ms.at[i], mr.at[i], partner)

    def multiply(i):
        band, o = STREAMS[i]
        count = 2

        def product(h):
            def step(t, carry):
                at = pl.ds(pl.multiple_of(t * (8 // count), 8 // count), 8 // count)
                right = cols[band, pl.ds(part_of(block_of(o), 0), 2)].reshape(local, half)
                left = rows[band, at, h].reshape(8 // count * sub, half)
                value = lax.dot_general(left, right, (((1,), (1,)), ((), ())), preferred_element_type=jnp.float32)
                scale = rq[at, h, :, 2 * band : 2 * band + 1].reshape(8 // count * sub, 1)
                value = value * scale * cq[o, 2 * band : 2 * band + 1]
                value = jnp.round(value).astype(jnp.int32).astype(jnp.int16)
                gram[i, h, at] = value.reshape(8 // count, sub, local)
                return carry

            lax.fori_loop(0, count, step, 0)

        product(1 - core)
        mate_copy(i).start()
        product(core)

    def start(i):
        mate_copy(i).wait_recv()
        for c, (turn, length, first, device) in enumerate(chains):
            ring[i, 7 + c] = own(i, toward(length, turn)).astype(jnp.int16)
            remote(ring.at[i, 7 + c], ring.at[i, first], zs.at[i, first], zr.at[i, first], device).start()

    def z_arrived(i, k):
        remote(ring.at[i, k], ring.at[i, k], zs.at[i, k], zr.at[i, k], onward).wait_recv()

    def own(i, d):
        return gram[i, core, d].astype(jnp.int32) + mate[i, d].astype(jnp.int32)

    def advance(i, step):
        band, o = STREAMS[i]
        for turn, length, first, device in chains:
            if step < length:
                k = first + step
                z_arrived(i, k - 1)
                total = ring[i, k - 1].astype(jnp.int32) + own(i, toward(length - step, turn))
                ring[i, k - 1] = total.astype(jnp.int16)
                remote(ring.at[i, k - 1], ring.at[i, k], zs.at[i, k], zr.at[i, k], device).start()
        if step < 4:
            return
        z_arrived(i, 3)
        z_arrived(i, 6)
        final = ring[i, 3].astype(jnp.int32) + ring[i, 6].astype(jnp.int32) + own(i, z)
        final = final.astype(jnp.float32)
        final = final * rq[z, core, :, 2 * band + 1 : 2 * band + 2] * cq[o, 2 * band + 1 : 2 * band + 2]
        o_ref[band, :, pl.ds(pl.multiple_of(block_of(o) * local, local), local)] = final

    def frame_sums():
        wide = lax.broadcasted_iota(jnp.int32, (sub, 128), 1)
        for t in range(4):
            at = pl.ds(t * sub, sub)
            columns = jnp.zeros((sub, 128), jnp.float32)
            for band in range(2):
                plain = jnp.zeros((sub, 128), jnp.float32)
                square = jnp.zeros((sub, 128), jnp.float32)
                for r in range(4):
                    flat = s[band, r, at, :] * gain(band, r)
                    plain = plain + flat
                    square = square + flat * flat
                columns = jnp.where(wide == 2 * band, jnp.sum(plain, axis=1, keepdims=True), columns)
                columns = jnp.where(wide == 2 * band + 1, jnp.sum(square, axis=1, keepdims=True), columns)
            s[0, 0, at, :] = columns
        pc[core] = jnp.transpose(s[0, 0])[:8]

    def scales(total):
        result = []
        for band in range(2):
            norm = jnp.sqrt(total[2 * band + 1 : 2 * band + 2])
            result += [(SCALE**0.5) / norm, norm * (pixels / (SCALE * pixels) ** 0.5) / total[2 * band : 2 * band + 1]]
        return jnp.concatenate([*result, jnp.zeros((4, local), jnp.float32)], axis=0)

    partner_sums = exchange(pc, core, [partner], pcs, pcr)
    z_sums = exchange(pz, z, z_peers, pzs, pzr)
    x_sums = exchange(rsum, tcol, x_peers, rss, rsr)
    y_sums = [remote(rsum, csum, css.at[i], csr.at[i], peer) for i, peer in enumerate(y_peers)]

    def tick(t):
        if t == 0:
            flatten(0)
            x_start(0, 0)
        if t in (1, 4):
            x_pass(t // 4)
        if t in (2, 5):
            for e in range(2):
                for h in range(2):
                    x_copy(1 - e, e, t // 4, h).wait_recv()
        if t in (3, 6):
            for e in range(2):
                for h in range(2):
                    x2_copy(e, t // 4, h).wait_recv()
        y_tick(t)
        if t in (2, 3):
            x_start(1, t - 2)
        if t == 0:
            x_start(0, 1)
            frame_sums()
            partner_sums[0].start()
            flatten(1)
            partner_sums[0].wait_recv()
            pz[z] = add_up(pc, 2)
            for copy in z_sums:
                copy.start()
        if t == 1:
            for copy in z_sums:
                copy.wait_recv()
            rsum[tcol] = scales(add_up(pz, 8))
            for copy in x_sums:
                copy.start()
        if t == 3:
            for copy in x_sums:
                copy.wait_recv()

            @pl.when(offset == 0)
            def _():
                for copy in y_sums:
                    copy.start()

            for block in range(4):
                tall = jnp.transpose(jnp.concatenate([rsum[block], jnp.zeros((120, local), jnp.float32)], axis=0))
                rq[2 * block : 2 * block + 2] = tall.reshape(2, 2, sub, 128)

    def take_sums():
        for i in range(3):
            @pl.when(offset == i + 1)
            def _():
                y_sums[i].wait_recv()

        for o in range(4):
            cq[o] = jnp.where(offset == 0, rsum[block_of(o)], csum[block_of(o)])

    for run in plan(tick, take_sums, y_arrived, multiply, start, advance):
        run()

    for i in range(8):
        mate_copy(i).wait_send()
    for band in range(2):
        for e in range(2):
            for h in range(2):
                x_copy(0, e, band, h).wait_send()
                x_copy(1, e, band, h).wait_send()
                x2_copy(e, band, h).wait_send()
    for d in range(2):
        @pl.when(position[d] < 3)
        def _():
            for i in range(7):
                for h in range(2):
                    y_next(d, i, h).wait_send()

        @pl.when(position[d] < 2)
        def _():
            for h in range(2):
                y_next(d, 7, h).wait_send()

        @pl.when(offset == 0)
        def _():
            for h in range(2):
                y_direct(d, h).wait_send()

    for copy in [*partner_sums, *z_sums, *x_sums]:
        copy.wait_send()

    @pl.when(offset == 0)
    def _():
        for copy in y_sums:
            copy.wait_send()

    def sent(step, carry):
        for i in range(8):
            remote(ring.at[i, step], ring.at[i, step], zs.at[i, step], zr.at[i, step], onward).wait_send()
        return carry

    lax.fori_loop(0, 7, sent, 0)


def per_device(frames, drift):
    local, _, tile_rows, columns = frames.shape
    total_frames = local * lax.axis_size("trow") * lax.axis_size("tcol")
    band_pixels = tile_rows * columns * lax.axis_size("pix")
    plain = frames.astype(jnp.bfloat16).transpose(1, 2, 0, 3)
    up = jnp.maximum(drift, 0).astype(jnp.float32) / 8.0
    down = jnp.maximum(-drift, 0).astype(jnp.float32) / 8.0
    stay = 1.0 - up - down
    weights = jnp.stack([stay[:, 0], up[:, 0], down[:, 0], stay[:, 1], up[:, 1], down[:, 1]], axis=1)

    dma = pltpu.SemaphoreType.DMA
    vmem = pl.BlockSpec(memory_space=pltpu.VMEM)
    block, half, sub = 4 * local, tile_rows * columns, local // 4
    f32, bf16, i16 = jnp.float32, jnp.bfloat16, jnp.int16
    out = pl.pallas_call(
        functools.partial(twotime_kernel, frames=float(total_frames), pixels=float(band_pixels)),
        out_shape=jax.ShapeDtypeStruct((2, block // 16, block), jnp.float32),
        in_specs=[vmem, vmem],
        out_specs=vmem,
        scratch_shapes=[
            pltpu.VMEM((2, 2, local, columns), bf16),
            pltpu.VMEM((2, tile_rows, local, columns), f32),
            pltpu.VMEM((2, 8, 2, sub, half), bf16),
            pltpu.VMEM((2, 8, 2, sub, half), bf16),
            pltpu.VMEM((8, 2, 8, sub, local), i16),
            pltpu.VMEM((8, 8, sub, local), i16),
            pltpu.VMEM((8, 9, sub, local), i16),
            pltpu.VMEM((4, 8, columns), f32),
            pltpu.VMEM((4, 8, columns), f32),
            pltpu.VMEM((2, 8, local), f32),
            pltpu.VMEM((8, 8, local), f32),
            pltpu.VMEM((4, 8, local), f32),
            pltpu.VMEM((4, 8, local), f32),
            pltpu.VMEM((8, 2, sub, 128), f32),
            pltpu.VMEM((4, 8, local), f32),
            dma((2,)), dma((2,)), dma((3,)), dma((3,)), dma((3,)), dma((3,)), dma((8,)), dma((8,)),
            dma((2, 2, 2, 2)), dma((2, 2, 2, 2)), dma((2, 2, 2)), dma((2, 2, 2)), dma((2, 8, 2)), dma((2, 8, 2)), dma((2, 8)), dma((2, 2)),
            dma((1,)), dma((1,)), dma((7,)), dma((7,)), dma((3,)), dma((3,)), dma((3,)), dma((3,)),
            dma((8, 7)), dma((8, 7)),
        ],
        compiler_params=pltpu.CompilerParams(collective_id=0, has_side_effects=True, vmem_limit_bytes=48 << 20),
        name="twotime",
    )(plain, weights)
    return out[0], out[1]


def solution(mesh):
    in_specs = (P(("trow", "tcol"), None, "pix", None), P(("trow", "tcol"), None))
    out_specs = (P(("trow", "pix"), "tcol"), P(("trow", "pix"), "tcol"))
    return jax.shard_map(
        per_device, mesh=mesh, in_specs=in_specs, out_specs=out_specs, check_vma=False
    )
```

```python
import functools

import jax
import jax.numpy as jnp
from jax import lax
from jax.experimental import pallas as pl
from jax.experimental.pallas import tpu as pltpu
from jax.sharding import PartitionSpec as P

MESH = pl.DeviceIdType.MESH
SCALE = 32000.0
OWN, WEST, EAST, FAR = range(4)
PATHS = tuple(
    tuple((o, band) for band in range(2) for o in blocks)
    for blocks in ((OWN, WEST, EAST, FAR), (OWN, EAST, WEST, FAR))
)
STREAMS = [(band, o) for band in range(2) for o in (OWN, WEST, EAST, FAR)]


def remote(src, dst, send, recv, device):
    return pltpu.make_async_remote_copy(
        src_ref=src, dst_ref=dst, send_sem=send, recv_sem=recv, device_id=device, device_id_type=MESH
    )


def around(index, step, count):
    return lax.rem(index + step + count, count)


def plan(tick, take_sums, y_arrived, multiply, start, advance):
    beat, hop, wire = 4.5, 3.0, 1.5
    todo = [(beat * t, 0, lambda t=t: tick(t)) for t in range(10)]
    ready = [beat * t for t in (4.4, 5.6, 5.7, 6.8, 7.6, 9.5, 9.6, 10.7)]
    clock, free, events = 0.0, 0.0, []
    for i, when in enumerate(ready):
        heads = [lambda: None]
        if i == 0:
            heads = [take_sums, lambda: y_arrived(0, 1)]
        elif i in (1, 3, 5, 7):
            heads = [lambda i=i: y_arrived(*((1, 3), (3, 4), (5, 7), (7, 8))[i // 2])]
        elif i == 4:
            heads = [lambda: y_arrived(4, 5)]
        for head in heads:
            todo.append((when, 1, head))
        todo.append((when, 2, lambda i=i: multiply(i)))
        events.append((when + 2.5, i, 0))
    while events:
        events.sort()
        when, i, step = events.pop(0)
        clock = max(clock + 0.3, when)
        todo.append((clock, 3, (lambda i=i: start(i)) if step == 0 else (lambda i=i, step=step: advance(i, step))))
        if step < 4:
            free = max(free, clock) + wire
            events.append((free + hop, i, step + 1))
    return [run for _, _, run in sorted(todo, key=lambda item: item[:2])]


def twotime_kernel(
    x_ref, w_ref, o_ref,
    halo, s, rows, cols, gram, mate, ring, px, py, pc, pz, rsum, csum, rq, cq,
    hs, hr, pxs, pxr, pys, pyr, ms, mr, xs, xr, x2s, x2r, ys, yr, yl, yd,
    pcs, pcr, pzs, pzr, rss, rsr, css, csr, zs, zr,
    *, frames, pixels,
):
    trow, tcol, pix = lax.axis_index("trow"), lax.axis_index("tcol"), lax.axis_index("pix")
    z, core = pix // 2, lax.rem(pix, 2)
    way = 1 - 2 * core
    local = x_ref.shape[2]
    sub = local // 4
    half = 4 * 128
    x_peers = [{"tcol": around(tcol, i, 4)} for i in (1, 2, 3)]
    y_peers = [{"trow": around(trow, i, 4)} for i in (1, 2, 3)]
    z_peers = [{"pix": around(pix, 2 * i, 16)} for i in range(1, 8)]
    east, west = x_peers[0], x_peers[2]
    south, north = y_peers[0], y_peers[2]
    onward, backward = {"pix": around(pix, 2 * way, 16)}, {"pix": around(pix, -2 * way, 16)}
    partner = {"pix": pix + way}
    other = {"pix": around(pix, -way, 16)}
    above, below = {"pix": around(pix, -1, 16)}, {"pix": around(pix, 1, 16)}

    barrier = pltpu.get_barrier_semaphore()
    for device in [*x_peers, *y_peers, *z_peers, partner, other]:
        pl.semaphore_signal(barrier, inc=1, device_id=device, device_id_type=MESH)
    pl.semaphore_wait(barrier, 15)

    edges = [
        remote(x_ref.at[:, 3], halo.at[0], hs.at[0], hr.at[0], below),
        remote(x_ref.at[:, 0], halo.at[1], hs.at[1], hr.at[1], above),
    ]
    for copy in edges:
        copy.start()
    lane = lax.broadcasted_iota(jnp.int32, (sub, 128), 1)
    has_above = (pix > 0).astype(jnp.float32)
    has_below = (pix < 15).astype(jnp.float32)
    sums = [[jnp.zeros((8, 128), jnp.float32) for _ in range(4)] for _ in range(2)]
    for inner in (True, False):
        if not inner:
            for copy in edges:
                copy.wait()
        for t in range(4):
            at = pl.ds(t * sub, sub)
            stay_r, up_r, down_r, stay_c, up_c, down_c = (w_ref[at, i : i + 1] for i in range(6))
            up_c = jnp.where(lane < 127, up_c, 0.0)
            down_c = jnp.where(lane > 0, down_c, 0.0)
            for band in range(2):
                line = {r + 1: x_ref[band, r, at, :].astype(jnp.float32) for r in range(4)}
                if not inner:
                    line[0] = halo[0, band, at, :].astype(jnp.float32) * has_above
                    line[5] = halo[1, band, at, :].astype(jnp.float32) * has_below
                for r in (1, 2) if inner else (0, 3):
                    mid = stay_r * line[r + 1] + up_r * line[r + 2] + down_r * line[r]
                    moved = stay_c * mid + up_c * pltpu.roll(mid, 127, 1) + down_c * pltpu.roll(mid, 1, 1)
                    s[band, r, at, :] = moved
                    sums[band][r] += jnp.sum(moved.reshape(sub // 8, 8, 128), axis=0)
    for band in range(2):
        for r in range(4):
            px[tcol, 4 * band + r] = jnp.sum(sums[band][r], axis=0)

    def exchange(slots, own, peers, send, recv):
        return [remote(slots.at[own], slots.at[own], send.at[i], recv.at[i], peer) for i, peer in enumerate(peers)]

    def add_up(slots, count):
        total = slots[0]
        for i in range(1, count):
            total = total + slots[i]
        return total

    def meet(slots, own, peers, send, recv):
        copies = exchange(slots, own, peers, send, recv)
        for copy in copies:
            copy.start()
        for copy in copies:
            copy.wait()
        return add_up(slots, len(peers) + 1)

    py[trow] = meet(px, tcol, x_peers, pxs, pxr)
    px[tcol] = frames / meet(py, trow, y_peers, pys, pyr)

    def gain(band, r):
        return px[tcol, pl.ds(4 * band + r, 1), :]

    def part_of(block, e):
        return 2 * block + e

    def flatten(band):
        for e in range(2):
            for h in range(2):
                at = pl.ds((2 * e + h) * sub, sub)
                for r in range(4):
                    flat = s[band, r, at, :] * gain(band, r)
                    rows[band, part_of(tcol, e), h, :, r * 128 : (r + 1) * 128] = flat.astype(jnp.bfloat16)

    def x_copy(d, e, band, h):
        place = rows.at[band, part_of(tcol, e), h]
        return remote(place, place, xs.at[d, e, band, h], xr.at[d, e, band, h], (east, west)[d])

    def x2_copy(e, band, h):
        place = rows.at[band, part_of(around(tcol, (-1, 1)[e], 4), e), h]
        return remote(place, place, x2s.at[e, band, h], x2r.at[e, band, h], (east, west)[e])

    offset = around(trow, -tcol, 4)
    position = (offset, around(0, -offset, 4))

    def block_of(o):
        return around(tcol, (0, -1, 1, 2)[o], 4)

    def y_copies(d, i):
        o, band = PATHS[d][i]
        here, there = rows.at[band, part_of(block_of(o), d)], cols.at[band, part_of(block_of(o), d)]
        device = (south, north)[d]
        return here, there, device, ys.at[d, i], yr.at[d, i]

    def y_next(d, i, h):
        _, there, device, send, recv = y_copies(d, i)
        return remote(there.at[h], there.at[h], send.at[h], recv.at[h], device)

    def y_stay(d, i):
        here, there, _, _, _ = y_copies(d, i)
        return pltpu.make_async_copy(here, there, yl.at[d, i])

    def y_direct(d, h):
        here, there, _, _, recv = y_copies(d, 7)
        return remote(here.at[h], there.at[h], yd.at[d, h], recv.at[h], (north, south)[d])

    def y_tick(tick):
        if tick < 8:
            @pl.when(offset == 0)
            def _():
                for h in range(2):
                    for d in range(2):
                        here, there, device, send, recv = y_copies(d, tick)
                        remote(here.at[h], there.at[h], send.at[h], recv.at[h], device).start()
                for d in range(2):
                    y_stay(d, tick).start()
                if tick == 7:
                    for d in range(2):
                        for h in range(2):
                            y_direct(d, h).start()

        for far in (1, 2):
            if 0 <= tick - far < 8:
                for h in range(2):
                    for d in range(2):
                        @pl.when(position[d] == far)
                        def _():
                            y_next(d, tick - far, h).wait_recv()
                            if (far, tick) != (2, 9):
                                y_next(d, tick - far, h).start()

    def y_arrived(first, last):
        for i in range(first, last):
            for d in range(2):
                @pl.when(position[d] == 3)
                def _():
                    for h in range(2):
                        y_next(d, i, h).wait_recv()

                @pl.when(position[d] == 0)
                def _():
                    y_stay(d, i).wait()

    def x_start(band, step):
        for h in range(2):
            for d in range(2):
                x_copy(d, (d + step) % 2, band, h).start()

    def x_pass(band):
        for h in range(2):
            for e in range(2):
                x_copy(e, e, band, h).wait_recv()
                x2_copy(e, band, h).start()

    chains = ((way, 4, 0, onward), (-way, 3, 4, backward))

    def toward(step, turn):
        return lax.rem(z + turn * step + 16, 8)

    def mate_copy(i):
        return remote(gram.at[i, 1 - core], mate.at[i], ms.at[i], mr.at[i], partner)

    def multiply(i):
        band, o = STREAMS[i]
        count = 1

        def product(h):
            def step(t, carry):
                at = pl.ds(pl.multiple_of(t * (8 // count), 8 // count), 8 // count)
                right = cols[band, pl.ds(part_of(block_of(o), 0), 2)].reshape(local, half)
                left = rows[band, at, h].reshape(8 // count * sub, half)
                value = lax.dot_general(left, right, (((1,), (1,)), ((), ())), preferred_element_type=jnp.float32)
                scale = rq[at, h, :, 2 * band : 2 * band + 1].reshape(8 // count * sub, 1)
                value = value * scale * cq[o, 2 * band : 2 * band + 1]
                value = jnp.round(value).astype(jnp.int32).astype(jnp.int16)
                gram[i, h, at] = value.reshape(8 // count, sub, local)
                return carry

            lax.fori_loop(0, count, step, 0)

        product(1 - core)
        mate_copy(i).start()
        product(core)

    def start(i):
        mate_copy(i).wait_recv()
        for c, (turn, length, first, device) in enumerate(chains):
            ring[i, 7 + c] = own(i, toward(length, turn)).astype(jnp.int16)
            remote(ring.at[i, 7 + c], ring.at[i, first], zs.at[i, first], zr.at[i, first], device).start()

    def z_arrived(i, k):
        remote(ring.at[i, k], ring.at[i, k], zs.at[i, k], zr.at[i, k], onward).wait_recv()

    def own(i, d):
        return gram[i, core, d].astype(jnp.int32) + mate[i, d].astype(jnp.int32)

    def advance(i, step):
        band, o = STREAMS[i]
        for turn, length, first, device in chains:
            if step < length:
                k = first + step
                z_arrived(i, k - 1)
                total = ring[i, k - 1].astype(jnp.int32) + own(i, toward(length - step, turn))
                ring[i, k - 1] = total.astype(jnp.int16)
                remote(ring.at[i, k - 1], ring.at[i, k], zs.at[i, k], zr.at[i, k], device).start()
        if step < 4:
            return
        z_arrived(i, 3)
        z_arrived(i, 6)
        final = ring[i, 3].astype(jnp.int32) + ring[i, 6].astype(jnp.int32) + own(i, z)
        final = final.astype(jnp.float32)
        final = final * rq[z, core, :, 2 * band + 1 : 2 * band + 2] * cq[o, 2 * band + 1 : 2 * band + 2]
        o_ref[band, :, pl.ds(pl.multiple_of(block_of(o) * local, local), local)] = final

    def frame_sums():
        wide = lax.broadcasted_iota(jnp.int32, (sub, 128), 1)
        for t in range(4):
            at = pl.ds(t * sub, sub)
            columns = jnp.zeros((sub, 128), jnp.float32)
            for band in range(2):
                plain = jnp.zeros((sub, 128), jnp.float32)
                square = jnp.zeros((sub, 128), jnp.float32)
                for r in range(4):
                    flat = s[band, r, at, :] * gain(band, r)
                    plain = plain + flat
                    square = square + flat * flat
                columns = jnp.where(wide == 2 * band, jnp.sum(plain, axis=1, keepdims=True), columns)
                columns = jnp.where(wide == 2 * band + 1, jnp.sum(square, axis=1, keepdims=True), columns)
            s[0, 0, at, :] = columns
        pc[core] = jnp.transpose(s[0, 0])[:8]

    def scales(total):
        result = []
        for band in range(2):
            norm = jnp.sqrt(total[2 * band + 1 : 2 * band + 2])
            result += [(SCALE**0.5) / norm, norm * (pixels / (SCALE * pixels) ** 0.5) / total[2 * band : 2 * band + 1]]
        return jnp.concatenate([*result, jnp.zeros((4, local), jnp.float32)], axis=0)

    partner_sums = exchange(pc, core, [partner], pcs, pcr)
    z_sums = exchange(pz, z, z_peers, pzs, pzr)
    x_sums = exchange(rsum, tcol, x_peers, rss, rsr)
    y_sums = [remote(rsum, csum, css.at[i], csr.at[i], peer) for i, peer in enumerate(y_peers)]

    def tick(t):
        if t == 0:
            flatten(0)
            x_start(0, 0)
        if t in (1, 4):
            x_pass(t // 4)
        if t in (2, 5):
            for e in range(2):
                for h in range(2):
                    x_copy(1 - e, e, t // 4, h).wait_recv()
        if t in (3, 6):
            for e in range(2):
                for h in range(2):
                    x2_copy(e, t // 4, h).wait_recv()
        y_tick(t)
        if t in (2, 3):
            x_start(1, t - 2)
        if t == 0:
            x_start(0, 1)
            frame_sums()
            partner_sums[0].start()
            flatten(1)
            partner_sums[0].wait_recv()
            pz[z] = add_up(pc, 2)
            for copy in z_sums:
                copy.start()
        if t == 1:
            for copy in z_sums:
                copy.wait_recv()
            rsum[tcol] = scales(add_up(pz, 8))
            for copy in x_sums:
                copy.start()
        if t == 3:
            for copy in x_sums:
                copy.wait_recv()

            @pl.when(offset == 0)
            def _():
                for copy in y_sums:
                    copy.start()

            for block in range(4):
                tall = jnp.transpose(jnp.concatenate([rsum[block], jnp.zeros((120, local), jnp.float32)], axis=0))
                rq[2 * block : 2 * block + 2] = tall.reshape(2, 2, sub, 128)

    def take_sums():
        for i in range(3):
            @pl.when(offset == i + 1)
            def _():
                y_sums[i].wait_recv()

        for o in range(4):
            cq[o] = jnp.where(offset == 0, rsum[block_of(o)], csum[block_of(o)])

    for run in plan(tick, take_sums, y_arrived, multiply, start, advance):
        run()

    for i in range(8):
        mate_copy(i).wait_send()
    for band in range(2):
        for e in range(2):
            for h in range(2):
                x_copy(0, e, band, h).wait_send()
                x_copy(1, e, band, h).wait_send()
                x2_copy(e, band, h).wait_send()
    for d in range(2):
        @pl.when(position[d] < 3)
        def _():
            for i in range(7):
                for h in range(2):
                    y_next(d, i, h).wait_send()

        @pl.when(position[d] < 2)
        def _():
            for h in range(2):
                y_next(d, 7, h).wait_send()

        @pl.when(offset == 0)
        def _():
            for h in range(2):
                y_direct(d, h).wait_send()

    for copy in [*partner_sums, *z_sums, *x_sums]:
        copy.wait_send()

    @pl.when(offset == 0)
    def _():
        for copy in y_sums:
            copy.wait_send()

    def sent(step, carry):
        for i in range(8):
            remote(ring.at[i, step], ring.at[i, step], zs.at[i, step], zr.at[i, step], onward).wait_send()
        return carry

    lax.fori_loop(0, 7, sent, 0)


def per_device(frames, drift):
    local, _, tile_rows, columns = frames.shape
    total_frames = local * lax.axis_size("trow") * lax.axis_size("tcol")
    band_pixels = tile_rows * columns * lax.axis_size("pix")
    plain = frames.astype(jnp.bfloat16).transpose(1, 2, 0, 3)
    up = jnp.maximum(drift, 0).astype(jnp.float32) / 8.0
    down = jnp.maximum(-drift, 0).astype(jnp.float32) / 8.0
    stay = 1.0 - up - down
    weights = jnp.stack([stay[:, 0], up[:, 0], down[:, 0], stay[:, 1], up[:, 1], down[:, 1]], axis=1)

    dma = pltpu.SemaphoreType.DMA
    vmem = pl.BlockSpec(memory_space=pltpu.VMEM)
    block, half, sub = 4 * local, tile_rows * columns, local // 4
    f32, bf16, i16 = jnp.float32, jnp.bfloat16, jnp.int16
    out = pl.pallas_call(
        functools.partial(twotime_kernel, frames=float(total_frames), pixels=float(band_pixels)),
        out_shape=jax.ShapeDtypeStruct((2, block // 16, block), jnp.float32),
        in_specs=[vmem, vmem],
        out_specs=vmem,
        scratch_shapes=[
            pltpu.VMEM((2, 2, local, columns), bf16),
            pltpu.VMEM((2, tile_rows, local, columns), f32),
            pltpu.VMEM((2, 8, 2, sub, half), bf16),
            pltpu.VMEM((2, 8, 2, sub, half), bf16),
            pltpu.VMEM((8, 2, 8, sub, local), i16),
            pltpu.VMEM((8, 8, sub, local), i16),
            pltpu.VMEM((8, 9, sub, local), i16),
            pltpu.VMEM((4, 8, columns), f32),
            pltpu.VMEM((4, 8, columns), f32),
            pltpu.VMEM((2, 8, local), f32),
            pltpu.VMEM((8, 8, local), f32),
            pltpu.VMEM((4, 8, local), f32),
            pltpu.VMEM((4, 8, local), f32),
            pltpu.VMEM((8, 2, sub, 128), f32),
            pltpu.VMEM((4, 8, local), f32),
            dma((2,)), dma((2,)), dma((3,)), dma((3,)), dma((3,)), dma((3,)), dma((8,)), dma((8,)),
            dma((2, 2, 2, 2)), dma((2, 2, 2, 2)), dma((2, 2, 2)), dma((2, 2, 2)), dma((2, 8, 2)), dma((2, 8, 2)), dma((2, 8)), dma((2, 2)),
            dma((1,)), dma((1,)), dma((7,)), dma((7,)), dma((3,)), dma((3,)), dma((3,)), dma((3,)),
            dma((8, 7)), dma((8, 7)),
        ],
        compiler_params=pltpu.CompilerParams(collective_id=0, has_side_effects=True, vmem_limit_bytes=48 << 20),
        name="twotime",
    )(plain, weights)
    return out[0], out[1]


def solution(mesh):
    in_specs = (P(("trow", "tcol"), None, "pix", None), P(("trow", "tcol"), None))
    out_specs = (P(("trow", "pix"), "tcol"), P(("trow", "pix"), "tcol"))
    return jax.shard_map(
        per_device, mesh=mesh, in_specs=in_specs, out_specs=out_specs, check_vma=False
    )
```
